32 devices in a mesh: cols: 8 (over y, x, core), vars: 4 (over z).
Axes of the slice: x: 2, y: 2, z: 4, core: 2. Of those that a mesh axis runs over, the one named last changes fastest.
Arguments:
- model_state: float32 [128, 4, 16, 72], P(('cols', 'vars')), may hold values from -6 to 6
- cloud_state: float32 [4, 50, 65536], P(None, None, ('cols', 'vars')), may hold values from -6 to 6
- neighbor: int32 [128, 4], P(('cols', 'vars')), may hold values from 0 to 127, as said below
- facing_edge: int32 [128, 4], P(('cols', 'vars')), may hold values from 0 to 3, as said below
- column_order: int32 [8, 256], P('cols'), may hold values from 0 to 255, each once within a row
- model_to_cloud_levels: float32 [50, 72], replicated, may hold values from -0.75 to 0.75
- cloud_to_model_levels: float32 [72, 50], replicated, may hold values from -0.875 to 0.875
Outputs:
- model_next: float32 [128, 4, 16, 72], P(('cols', 'vars'))
- cloud_next: float32 [4, 50, 65536], P(None, None, ('cols', 'vars'))
The draws below stay inside these ranges and needn't reach their ends.
Inputs may be any that keep to these rules, and one draw needn't show every extreme that they name: neighbor[e,j] is the element across edge j of element e; it lies in the same block of 4 consecutive elements as e or in one of the two blocks beside it, the first and last blocks counting as beside each other. Neighbours are mutual: if edge j of e faces edge f = facing_edge[e,j] of b, then edge f of b faces edge j of e. facing_edge[e,j] is the edge of neighbor[e,j] that edge j of e faces; the shared edge's nodes run in opposite orders in the two elements. `column_order`: each row is a permutation.
All inputs are finite; a program needn't handle non-finite values.
Results may differ from the reference program's by a relative error of at most 0.0003.
Values sent between devices are 32-bit elements; how exact they have to be, the bound alone decides.
No kernel may reach another device: no remote copies, remote signals or barrier semaphores. Data moves between devices by JAX's collectives and lax.ppermute only.
A program may use at most 128 MiB of HBM per device.

```python
import jax
import jax.numpy as jnp
import numpy as np
from jax import lax

NPTS = 16
LEV = 72
CLEV = 50
CCOL = 32
NVAR = 4
ELEM_DEV = 4
NE = 128
COL_DEV = 256
GROUPS = 8
NCOL = 2048
N_COLS = 8


STEPS_AROUND = [(-1, 0), (0, 1), (1, 0), (0, -1)]


def mesh_tables(key):
    row_count = NE // ELEM_DEV
    key_order, key_turn = jax.random.split(jax.random.fold_in(key, 811))
    shuffled = jax.vmap(lambda subkey: jax.random.permutation(subkey, ELEM_DEV))(jax.random.split(key_order, row_count))
    element_ids = (jnp.arange(row_count, dtype=jnp.int32)[:, None] * ELEM_DEV + shuffled.astype(jnp.int32)).astype(jnp.int32)
    rotation = jax.random.randint(key_turn, (NE,), 0, 4).astype(jnp.int32)
    adjacent = jnp.stack([jnp.roll(element_ids, (-vertical, -sideways), axis=(0, 1)) for vertical, sideways in STEPS_AROUND], axis=-1)
    canonical = jnp.arange(4, dtype=jnp.int32)
    own_edge = (canonical + rotation[element_ids][..., None]) % 4
    far_edge = ((canonical + 2) % 4 + rotation[adjacent]) % 4
    owners = jnp.broadcast_to(element_ids[..., None], adjacent.shape).reshape(-1)
    neighbor = jnp.zeros((NE, 4), jnp.int32).at[owners, own_edge.reshape(-1)].set(adjacent.reshape(-1))
    facing_edge = jnp.zeros((NE, 4), jnp.int32).at[owners, own_edge.reshape(-1)].set(far_edge.reshape(-1).astype(jnp.int32))
    return (neighbor, facing_edge)


def draw_neighbor(key, part):
    return mesh_tables(key)[0]


def draw_facing_edge(key, part):
    return mesh_tables(key)[1]


def steps_of(key, dims, shards, least, high):
    level = 1.0
    for axis_at, blocks in shards:
        heights = jax.random.uniform(jax.random.fold_in(jax.random.fold_in(key, 6), axis_at), (blocks,), jnp.float32, least / len(shards), high / len(shards))
        level = level * jnp.repeat(jnp.exp(heights), dims[axis_at] // blocks).reshape((-1,) + (1,) * (len(dims) - 1 - axis_at))
    return level


def normal_values(key, extent, deviation, limit, cuts=(), held_as=jnp.bfloat16):
    level = steps_of(key, extent, cuts, -0.22, 0.18) if cuts else 1.0
    values = jax.random.normal(key, extent, jnp.float32) * deviation * level
    return jnp.minimum(jnp.maximum(values, -limit), limit).astype(held_as)


def setup_inputs(seed: int = 0) -> dict:
    splits = jax.random.split(jax.random.key(seed), 8)
    return {
        "model_state": normal_values(splits[0], (NE, NVAR, NPTS, LEV), 1.0, 6.0, ((0, 32),), jnp.float32),
        "cloud_state": normal_values(splits[1], (NVAR, CLEV, NCOL * CCOL), 1.0, 6.0, ((2, 32),), jnp.float32),
        "neighbor": draw_neighbor(jax.random.fold_in(splits[7], 71), 0),
        "facing_edge": draw_facing_edge(jax.random.fold_in(splits[7], 71), 0),
        "column_order": jax.vmap(lambda own: jax.random.permutation(own, COL_DEV))(jax.random.split(splits[4], GROUPS)).reshape((GROUPS, COL_DEV)).astype(jnp.int32),
        "model_to_cloud_levels": normal_values(splits[5], (CLEV, LEV), LEV ** -0.5, 0.75, (), jnp.float32),
        "cloud_to_model_levels": normal_values(splits[6], (LEV, CLEV), CLEV ** -0.5, 0.875, (), jnp.float32),
    }


TOP_LEVEL_INDEX = lax.Precision.HIGHEST
VISCOSITY = 0.01
DRIFT = 0.05
PENALTY = 0.5
TIME_STEP = 0.5
CLOUD_ADVECT = 0.25
CLOUD_DIFFUSE = 0.1
CONDENSE_RATE = 0.3
SATURATION_BASE = 0.5
SATURATION_SLOPE = 0.3
RETAIN = 0.8
EDGE_NODES = [[0, 1, 2, 3], [3, 7, 11, 15], [15, 14, 13, 12], [12, 8, 4, 0]]

def lobatto_derivative():
    points = np.array([-1.0, -1.0 / np.sqrt(5.0), 1.0 / np.sqrt(5.0), 1.0])
    derivative = np.zeros((4, 4))
    for target in range(4):
        for source in range(4):
            if target != source:
                weight_target = np.prod([points[target] - points[middle] for middle in range(4) if middle != target])
                weight_source = np.prod([points[source] - points[middle] for middle in range(4) if middle != source])
                derivative[target, source] = weight_target / (weight_source * (points[target] - points[source]))
        derivative[target, target] = np.sum([1.0 / (points[target] - points[middle]) for middle in range(4) if middle != target])
    return derivative

def node_operators():
    derivative = lobatto_derivative()
    identity = np.eye(4)
    along_first = np.kron(identity, derivative)
    along_second = np.kron(derivative, identity)
    laplace = along_first @ along_first + along_second @ along_second
    return (jnp.asarray(along_first, jnp.float32), jnp.asarray(laplace, jnp.float32))

def edge_tables():
    source = np.zeros((4, 4, 16))
    target = np.zeros((4, 4, 16))
    for edge in range(4):
        for place in range(4):
            source[edge, place, EDGE_NODES[edge][3 - place]] = 1.0
            target[edge, place, EDGE_NODES[edge][place]] = 1.0
    return (jnp.asarray(source, jnp.float32), jnp.asarray(target, jnp.float32))

def tendency_of(own_elems, far_list, facing_edge):
    along_first, laplace = node_operators()
    source, target = edge_tables()
    diffused = jnp.einsum('mn,evnl->evml', laplace, own_elems, precision=TOP_LEVEL_INDEX)
    slope = jnp.einsum('mn,evnl->evml', along_first, own_elems, precision=TOP_LEVEL_INDEX)
    result = VISCOSITY * diffused - DRIFT * own_elems[:, 3:4] * slope
    penalty_sum = jnp.zeros_like(own_elems)
    for edge in range(4):
        choose = (facing_edge[:, edge][:, None] == jnp.arange(4, dtype=jnp.int32)[None, :]).astype(jnp.float32)
        picker = jnp.einsum('ef,ftn->etn', choose, source, precision=TOP_LEVEL_INDEX)
        facing = jnp.einsum('etn,evnl->evtl', picker, far_list[edge], precision=TOP_LEVEL_INDEX)
        inside = jnp.einsum('tn,evnl->evtl', target[edge], own_elems, precision=TOP_LEVEL_INDEX)
        penalty_sum = penalty_sum + jnp.einsum('tm,evtl->evml', target[edge], facing - inside, precision=TOP_LEVEL_INDEX)
    return result + PENALTY * penalty_sum

def cloud_step(cloud_fields, applied_forcing):
    cloud_wind = cloud_fields[3:4]
    advect = -CLOUD_ADVECT * cloud_wind * (jnp.roll(cloud_fields, -1, axis=2) - jnp.roll(cloud_fields, 1, axis=2))
    padded = jnp.pad(cloud_fields, ((0, 0), (1, 1), (0, 0), (0, 0)))
    diffuse = CLOUD_DIFFUSE * (padded[:, 2:] - 2.0 * cloud_fields + padded[:, :-2])
    moved = cloud_fields + TIME_STEP * (advect + diffuse + applied_forcing)
    saturation = SATURATION_BASE * jnp.exp(SATURATION_SLOPE * moved[0])
    condensed = CONDENSE_RATE * jax.nn.softplus(moved[1] - saturation)
    updated = jnp.stack([moved[0] + condensed, moved[1] - condensed, RETAIN * moved[2] + condensed, moved[3]])
    state_increment = lax.optimization_barrier(jnp.mean(updated - cloud_fields, axis=2, keepdims=True)) / TIME_STEP
    return (updated, state_increment)

def reference(model_state, cloud_state, neighbor, facing_edge, column_order, model_to_cloud_levels, cloud_to_model_levels):
    cloud_view = cloud_state.reshape(NVAR, CLEV, NCOL, CCOL).transpose(0, 1, 3, 2)
    far_list = [jnp.take(model_state, neighbor[:, edge], axis=0) for edge in range(4)]
    tendency = tendency_of(model_state, far_list, facing_edge)
    dyn_cols = jnp.transpose(tendency, (1, 3, 0, 2)).reshape(NVAR, LEV, NE * 16)
    positions = jnp.arange(NCOL, dtype=jnp.int32)
    group = positions // COL_DEV
    slot = column_order.reshape(-1).astype(jnp.int32)
    share = COL_DEV // N_COLS
    source_col = (slot // share * COL_DEV + group * share + slot % share).astype(jnp.int32)
    positioned_blocks = jnp.take(dyn_cols, source_col, axis=2)
    applied_forcing = jnp.einsum('dg,wgk->wdk', model_to_cloud_levels, positioned_blocks, precision=TOP_LEVEL_INDEX)[:, :, None, :]

    def one_block(block):
        begin = (block * COL_DEV).astype(jnp.int32)
        fields = lax.dynamic_slice_in_dim(cloud_view, begin, COL_DEV, 3)
        pushed = lax.dynamic_slice_in_dim(applied_forcing, begin, COL_DEV, 3)
        return cloud_step(fields, pushed)
    new_blocks, change_blocks = lax.map(one_block, jnp.arange(N_COLS, dtype=jnp.int32))
    cloud_next = jnp.moveaxis(new_blocks, 0, 3).reshape(NVAR, CLEV, CCOL, NCOL)
    cloud_next = cloud_next.transpose(0, 1, 3, 2).reshape(NVAR, CLEV, NCOL * CCOL)
    state_increment = jnp.moveaxis(change_blocks, 0, 3).reshape(NVAR, CLEV, NCOL)
    returned_output = jnp.einsum('xi,yie->yxe', cloud_to_model_levels, state_increment, precision=TOP_LEVEL_INDEX)
    feedback_cols = jnp.zeros_like(returned_output).at[:, :, source_col].set(returned_output)
    feedback = feedback_cols.reshape(NVAR, LEV, NE, 16).transpose(2, 0, 3, 1)
    model_next = model_state + TIME_STEP * (tendency + feedback)
    return (model_next, cloud_next)
```

```python
import functools

import jax
import jax.numpy as jnp
import numpy as np
from jax import lax
from jax.experimental import pallas as pl
from jax.experimental.pallas import tpu as pltpu
from jax.sharding import PartitionSpec as P

CCOL = 32
NODES = 16
LANES = 128
ROWS = 8
AXES = ("cols", "vars")
VISCOSITY = 0.01
DRIFT = 0.05
PENALTY = 0.5
TIME_STEP = 0.5
CLOUD_ADVECT = 0.25
CLOUD_DIFFUSE = 0.1
CONDENSE_RATE = 0.3
SATURATION_BASE = 0.5
SATURATION_SLOPE = 0.3
RETAIN = 0.8
EXACT = lax.Precision.HIGHEST
FAR_ROW = 6
ORDER_ROW = 7


def lobatto_derivative():
    points = np.array([-1.0, -1.0 / np.sqrt(5.0), 1.0 / np.sqrt(5.0), 1.0])
    derivative = np.zeros((4, 4))
    for target in range(4):
        for source in range(4):
            if target != source:
                weight_target = np.prod(
                    [points[target] - points[middle] for middle in range(4) if middle != target]
                )
                weight_source = np.prod(
                    [points[source] - points[middle] for middle in range(4) if middle != source]
                )
                derivative[target, source] = weight_target / (
                    weight_source * (points[target] - points[source])
                )
        derivative[target, target] = np.sum(
            [1.0 / (points[target] - points[middle]) for middle in range(4) if middle != target]
        )
    return derivative


def node_weights():
    derivative = lobatto_derivative()
    along_first = np.kron(np.eye(4), derivative)
    along_second = np.kron(derivative, np.eye(4))
    laplace = along_first @ along_first + along_second @ along_second
    edges = np.zeros((4, 4))
    edges[0, :] += 1.0
    edges[3, :] += 1.0
    edges[:, 0] += 1.0
    edges[:, 3] += 1.0
    linear = VISCOSITY * laplace - PENALTY * np.diag(edges.reshape(-1))
    repeat = np.eye(LANES // NODES)
    return np.concatenate(
        [np.kron(repeat, linear.T), np.kron(repeat, -DRIFT * along_first.T)], axis=1
    ).astype(np.float32)


def each(count, body):
    if count <= 16:
        for index in range(count):
            body(index)
    else:
        lax.fori_loop(0, count, lambda index, carry: (body(index), carry)[1], 0)


def lane_ids(rows=ROWS):
    return lax.broadcasted_iota(jnp.int32, (rows, LANES), 1)


def row_ids():
    return lax.broadcasted_iota(jnp.int32, (ROWS, LANES), 0)


def pick(values, lanes):
    return jnp.take_along_axis(values, lanes, axis=1, mode="promise_in_bounds")


def half_turn(values):
    return pltpu.roll(values, LANES // 2, 1)


def split_pair(first, second):
    lower = lane_ids() < LANES // 2
    return (
        jnp.where(lower, first, half_turn(second)),
        jnp.where(lower, half_turn(first), second),
    )


def row_of(values, row):
    return jnp.broadcast_to(values[row : row + 1], (ROWS, LANES))


def pack_kernel(own_ref, nbr_ref, face_ref, order_ref, state_ref, out_ref, scratch, depth, block):
    elements, variables, nodes, levels = state_ref.shape
    used = levels // depth
    half = LANES // 2
    lane = lane_ids()
    own = own_ref[0]
    column = lane % half
    elem = column // nodes
    along_y = (column // 4) % 4
    along_x = column % 4
    upper = lane >= half
    edge = jnp.where(
        upper,
        jnp.where(along_x == 3, 1, jnp.where(along_x == 0, 3, -1)),
        jnp.where(along_y == 0, 0, jnp.where(along_y == 3, 2, -1)),
    )
    along = jnp.where(upper, along_y, along_x)
    place = jnp.where(edge >= 2, 3 - along, along)
    far = jnp.zeros_like(lane)
    face = jnp.zeros_like(lane)
    for e in range(elements):
        for j in range(4):
            here = (elem == e) & (edge == j)
            far = jnp.where(here, nbr_ref[e, j], far)
            face = jnp.where(here, face_ref[e, j], face)
    node = jnp.where(
        face == 0,
        3 - place,
        jnp.where(face == 1, 15 - 4 * place, jnp.where(face == 2, 12 + place, 4 * place)),
    )
    far_col = jnp.where(edge >= 0, nodes * far + node, -1).astype(jnp.float32)

    order = order_ref[...]
    spots = lax.broadcasted_iota(jnp.int32, (block, block), 0)
    marks = (spots == order).astype(jnp.float32).astype(jnp.bfloat16)
    numbers = lax.broadcasted_iota(jnp.int32, (ROWS, block), 1).astype(jnp.float32)
    scratch[0] = jnp.broadcast_to(order, (ROWS, block)).astype(jnp.float32)
    scratch[1] = lax.dot_general(
        numbers.astype(jnp.bfloat16),
        marks,
        (((1,), (1,)), ((), ())),
        preferred_element_type=jnp.float32,
    )
    begin = pl.multiple_of((own // 2) * LANES, LANES)
    order_part = scratch[0, :, pl.ds(begin, LANES)]
    place_part = scratch[1, :, pl.ds(begin, LANES)]
    odd = own % 2 == 1
    order_part = jnp.where(odd, half_turn(order_part), order_part)
    place_part = jnp.where(odd, place_part, half_turn(place_part))
    indices = jnp.where(upper, place_part, order_part)

    out_ref[...] = jnp.zeros_like(out_ref)
    slots = out_ref.shape[0] // ROWS
    for first in range(0, slots, ROWS):
        out_ref[pl.ds(ROWS * first + FAR_ROW, ROWS, stride=ROWS), :] = far_col
        out_ref[pl.ds(ROWS * first + ORDER_ROW, ROWS, stride=ROWS), :] = indices
    for pair in range(variables // 2):
        fields = jnp.concatenate(
            [
                state_ref[:, pair].reshape(elements * nodes, levels),
                state_ref[:, variables // 2 + pair].reshape(elements * nodes, levels),
            ],
            axis=0,
        )
        by_level = fields.T
        for part in range(depth):
            for first in range(0, used, ROWS):
                begin = used * part + first
                out_ref[pl.ds(ROWS * first + depth * pair + part, ROWS, stride=ROWS), :] = (
                    by_level[begin : begin + ROWS]
                )


def tendency_kernel(got_ref, weight_ref, out_ref, partial_ref, field, linear, tend, depth, share):
    tiles = field.shape[0]
    block = LANES * 2
    tiles_block = block // LANES
    col_count = block // share
    lane = lane_ids()
    row = row_ids()
    lower = lane < LANES // 2

    def unpack(q):
        low, high = split_pair(got_ref[2 * q], got_ref[2 * q + 1])
        field[q, 0] = low
        field[q, 1] = high

    each(tiles, unpack)

    step = min(tiles, 16)

    def multiply(chunk):
        fields = field[pl.ds(chunk * step, step)].reshape(step * 2 * ROWS, LANES)
        result = jnp.dot(fields, weight_ref[...], precision=EXACT)
        linear[pl.ds(chunk * step, step)] = result.reshape(step, 2, ROWS, 2 * LANES)

    each(tiles // step, multiply)

    def advance(q):
        before = (q + tiles - 1) % tiles
        after = (q + 1) % tiles
        high = field[q, 1]
        wind = jnp.where(row < depth, pltpu.roll(high, ROWS - depth, 0), high)
        sums = [jnp.zeros((ROWS, LANES), jnp.float32)] * 2
        for side in range(2):
            far = row_of(field[q, side], FAR_ROW).astype(jnp.int32)
            spot = jnp.maximum(far, 0) % LANES
            inside = far // LANES == q
            for part in range(2):
                beside = jnp.where(lower, field[after, part], field[before, part])
                value = jnp.where(inside, pick(field[q, part], spot), pick(beside, spot))
                sums[part] = sums[part] + jnp.where(far >= 0, value, 0.0)
        for part in range(2):
            own = field[q, part]
            result = (
                linear[q, part, :, :LANES]
                + wind * linear[q, part, :, LANES:]
                + PENALTY * sums[part]
            )
            tend[q, part] = result
            partial_ref[q, part] = jnp.where(row < FAR_ROW, own + TIME_STEP * result, own)

    each(tiles, advance)

    def arrange(p):
        col = p // tiles_block
        order = row_of(field[p, 0], ORDER_ROW).astype(jnp.int32)
        owner = order // share
        spot = (share * col) % LANES + order % share
        base = (share * col) // LANES
        parts = [jnp.zeros((ROWS, LANES), jnp.float32)] * 2
        for k in range(col_count):
            for part in range(2):
                source = tend[tiles_block * k + base, part]
                parts[part] = jnp.where(owner == k, pick(source, spot), parts[part])
        first, second = split_pair(parts[0], parts[1])
        out_ref[2 * p] = first
        out_ref[2 * p + 1] = second

    each(tiles, arrange)


def cloud_kernel(
    got_ref, down_ref, up_ref, cloud_ref, next_ref, out_ref, forced, pooled, depth, levels
):
    clev, variables, width = cloud_ref.shape
    used = levels // depth
    lane = lane_ids()
    row = row_ids()
    half = LANES // 2
    lower = lane < half
    rows = clev * variables
    for pair in range(2):
        fields = jnp.concatenate(
            [
                got_ref[pl.ds(ROWS * first + depth * pair + part, ROWS, stride=ROWS), :]
                for part in range(depth)
                for first in range(0, used, ROWS)
            ],
            axis=0,
        )
        forcing = TIME_STEP * jnp.dot(down_ref[...], fields, precision=EXACT)
        turned = half_turn(forcing)
        for first in range(0, clev, ROWS):
            count = min(ROWS, clev - first)
            forced[pl.ds(variables * first + pair, count, stride=variables), :] = forcing[
                first : first + count
            ]
            forced[pl.ds(variables * first + 2 + pair, count, stride=variables), :] = turned[
                first : first + count
            ]
    pooled[...] = jnp.zeros_like(pooled)
    within = lane % CCOL
    var = row % variables
    wind_row = (row // variables) * variables + 3
    lead_row = (row // variables) * variables
    keep = jnp.where(var == 2, RETAIN, 1.0).astype(jnp.float32)
    sign = jnp.where(var == 1, -1.0, jnp.where(var == 3, 0.0, 1.0)).astype(jnp.float32)
    first_half = row < variables
    pool_lane = lax.broadcasted_iota(jnp.int32, (LANES, LANES), 1) % half
    pool_row = lax.broadcasted_iota(jnp.int32, (LANES, LANES), 0) // CCOL
    pairs = clev // 2

    def tile(t, carry):
        begin = pl.multiple_of(t * LANES, LANES)

        def load(a):
            return cloud_ref[2 * a : 2 * a + 2, :, pl.ds(begin, LANES)].reshape(ROWS, LANES)

        spread = (LANES // CCOL) * t + lane // CCOL
        zero = jnp.zeros((ROWS, LANES), jnp.float32)
        turned_before = zero
        now = load(0)
        turned = pltpu.roll(now, variables, 0)
        changes = []
        for a in range(pairs):
            following = load(a + 1) if a + 1 < pairs else zero
            turned_after = pltpu.roll(following, variables, 0) if a + 1 < pairs else zero
            above = jnp.where(first_half, turned, turned_after)
            below = jnp.where(first_half, turned_before, turned)
            ahead = jnp.where(
                within == CCOL - 1, pltpu.roll(now, CCOL - 1, 1), pltpu.roll(now, LANES - 1, 1)
            )
            behind = jnp.where(
                within == 0, pltpu.roll(now, LANES - CCOL + 1, 1), pltpu.roll(now, 1, 1)
            )
            wind = jnp.take_along_axis(now, wind_row, axis=0, mode="promise_in_bounds")
            advect = (-CLOUD_ADVECT * TIME_STEP) * wind * (ahead - behind)
            diffuse = (CLOUD_DIFFUSE * TIME_STEP) * (above - 2.0 * now + below)
            push = pick(forced[ROWS * a : ROWS * a + ROWS, :], spread)
            moved = now + (advect + diffuse + push)
            excess = pltpu.roll(moved, ROWS - 1, 0) - SATURATION_BASE * jnp.exp(
                SATURATION_SLOPE * moved
            )
            soft = jnp.maximum(excess, 0.0) + jnp.log1p(jnp.exp(-jnp.abs(excess)))
            condensed = CONDENSE_RATE * jnp.take_along_axis(
                soft, lead_row, axis=0, mode="promise_in_bounds"
            )
            updated = keep * moved + sign * condensed
            next_ref[2 * a : 2 * a + 2, :, pl.ds(begin, LANES)] = updated.reshape(
                2, variables, LANES
            )
            changes.append(updated - now)
            turned_before, turned, now = turned, turned_after, following
        change = jnp.concatenate(changes, axis=0)
        pool = jnp.where(
            pool_lane == (LANES // CCOL) * t + pool_row, 1.0 / (CCOL * TIME_STEP), 0.0
        ).astype(jnp.float32)
        pooled[...] += jnp.dot(change, pool, precision=EXACT)
        return carry

    lax.fori_loop(0, width // LANES, tile, 0)
    for pair in range(2):
        mean = jnp.where(
            lane_ids(clev) < half,
            pooled[pl.ds(pair, clev, stride=variables), :],
            pooled[pl.ds(2 + pair, clev, stride=variables), :],
        )
        feedback = jnp.dot(up_ref[...], mean, precision=EXACT)
        for part in range(depth):
            for first in range(0, used, ROWS):
                begin = used * part + first
                out_ref[pl.ds(ROWS * first + depth * pair + part, ROWS, stride=ROWS), :] = (
                    feedback[begin : begin + ROWS]
                )


def update_kernel(got_ref, partial_ref, out_ref, field, share):
    tiles = field.shape[0]
    block = LANES * 2
    tiles_block = block // LANES
    lane = lane_ids()
    groups = LANES // share
    group = lane // share
    inner = lane % share

    def unpack(p):
        low, high = split_pair(got_ref[2 * p], got_ref[2 * p + 1])
        field[p, 0] = low
        field[p, 1] = high

    each(tiles, unpack)

    def collect(q):
        k = q // tiles_block
        start = (LANES * (q % tiles_block)) // share
        offset = share * k
        place = jnp.zeros((ROWS, LANES), jnp.float32)
        for g in range(groups):
            source = row_of(partial_ref[tiles_block * (start + g) + offset // LANES, 1], ORDER_ROW)
            place = jnp.where(group == g, pick(source, offset % LANES + inner), place)
        place = place.astype(jnp.int32)
        spot = place % LANES
        parts = [jnp.zeros((ROWS, LANES), jnp.float32)] * 2
        for g in range(groups):
            for piece in range(tiles_block):
                chosen = (group == g) & (place // LANES == piece)
                for part in range(2):
                    source = field[tiles_block * (start + g) + piece, part]
                    parts[part] = jnp.where(chosen, pick(source, spot), parts[part])
        low = partial_ref[q, 0] + TIME_STEP * parts[0]
        high = partial_ref[q, 1] + TIME_STEP * parts[1]
        first, second = split_pair(low, high)
        out_ref[2 * q] = first
        out_ref[2 * q + 1] = second

    each(tiles, collect)


def unpack_kernel(got_ref, state_ref, depth):
    elements, variables, nodes, levels = state_ref.shape
    used = levels // depth
    for pair in range(variables // 2):
        by_level = jnp.concatenate(
            [
                got_ref[pl.ds(ROWS * first + depth * pair + part, ROWS, stride=ROWS), :]
                for part in range(depth)
                for first in range(0, used, ROWS)
            ],
            axis=0,
        )
        fields = by_level.T.reshape(2, elements, nodes, levels)
        state_ref[:, pair] = fields[0]
        state_ref[:, variables // 2 + pair] = fields[1]


def kernel_call(body, name, results, scratch, *operands, spaces=None):
    vmem = pl.BlockSpec(memory_space=pltpu.VMEM)
    smem = pl.BlockSpec(memory_space=pltpu.SMEM)
    return pl.pallas_call(
        body,
        name=name,
        out_shape=results,
        in_specs=[smem if spaces and n in spaces else vmem for n in range(len(operands))],
        out_specs=jax.tree.map(lambda _: vmem, results),
        scratch_shapes=scratch,
    )(*operands)


def exchange(slots):
    return lax.all_to_all(slots, AXES, split_axis=0, concat_axis=0, tiled=True)


def shards(
    model_state,
    cloud_state,
    neighbor,
    facing_edge,
    column_order,
    model_to_cloud_levels,
    cloud_to_model_levels,
):
    elements, variables, nodes, levels = model_state.shape
    clev, width = cloud_state.shape[1:]
    devices = lax.axis_size(AXES)
    block = column_order.shape[1]
    share = block // lax.axis_size("cols")
    depth = -(-levels // devices)
    assert variables == 4 and nodes == NODES and 2 * elements * nodes == LANES
    assert 2 * depth <= FAR_ROW and levels % (ROWS * depth) == 0 and block == 2 * LANES
    tiles = devices // 2
    f32 = jnp.float32
    shape = jax.ShapeDtypeStruct
    flat = shape((devices * ROWS, LANES), f32)
    slots = shape((devices, ROWS, LANES), f32)
    pairs = shape((tiles, 2, ROWS, LANES), f32)
    own = lax.axis_index("vars").astype(jnp.int32).reshape(1)

    packed = kernel_call(
        functools.partial(pack_kernel, depth=depth, block=block),
        "pack_state",
        flat,
        [pltpu.VMEM((2, ROWS, block), f32)],
        own,
        neighbor,
        facing_edge,
        column_order,
        model_state,
        spaces=(0, 1, 2),
    )
    by_level = exchange(packed.reshape(slots.shape))
    arranged, partial = kernel_call(
        functools.partial(tendency_kernel, depth=depth, share=share),
        "tendency",
        (slots, pairs),
        [
            pltpu.VMEM(pairs.shape, f32),
            pltpu.VMEM((tiles, 2, ROWS, 2 * LANES), f32),
            pltpu.VMEM(pairs.shape, f32),
        ],
        by_level,
        jnp.asarray(node_weights()),
    )
    by_column = exchange(arranged)
    cloud_next, fed = kernel_call(
        functools.partial(cloud_kernel, depth=depth, levels=levels),
        "cloud",
        (shape((clev, variables, width), f32), flat),
        [
            pltpu.VMEM((clev * variables, LANES), f32),
            pltpu.VMEM((clev * variables, LANES), f32),
        ],
        by_column.reshape(flat.shape),
        model_to_cloud_levels,
        cloud_to_model_levels,
        jnp.transpose(cloud_state, (1, 0, 2)),
    )
    fed_level = exchange(fed.reshape(slots.shape))
    advanced = kernel_call(
        functools.partial(update_kernel, share=share),
        "update",
        slots,
        [pltpu.VMEM(pairs.shape, f32)],
        fed_level,
        partial,
    )
    home = exchange(advanced)
    model_next = kernel_call(
        functools.partial(unpack_kernel, depth=depth),
        "unpack_state",
        shape(model_state.shape, f32),
        [],
        home.reshape(flat.shape),
    )
    return (model_next, jnp.transpose(cloud_next, (1, 0, 2)))


def solution(mesh):
    placed = (
        P(AXES, None, None, None),
        P(None, None, AXES),
        P(AXES, None),
        P(AXES, None),
        P("cols", None),
        P(),
        P(),
    )
    return jax.shard_map(
        shards,
        mesh=mesh,
        in_specs=placed,
        out_specs=(P(AXES, None, None, None), P(None, None, AXES)),
        check_vma=False,
    )
```

```python
import functools

import jax
import jax.numpy as jnp
import numpy as np
from jax import lax
from jax.experimental import pallas as pl
from jax.experimental.pallas import tpu as pltpu
from jax.sharding import PartitionSpec as P

CCOL = 32
NODES = 16
LANES = 128
ROWS = 8
AXES = ("cols", "vars")
VISCOSITY = 0.01
DRIFT = 0.05
PENALTY = 0.5
TIME_STEP = 0.5
CLOUD_ADVECT = 0.25
CLOUD_DIFFUSE = 0.1
CONDENSE_RATE = 0.3
SATURATION_BASE = 0.5
SATURATION_SLOPE = 0.3
RETAIN = 0.8
EXACT = lax.Precision.HIGHEST
KERNEL_VMEM = 16 * 2**20
FAR_ROW = 6
ORDER_ROW = 7


def lobatto_derivative():
    points = np.array([-1.0, -1.0 / np.sqrt(5.0), 1.0 / np.sqrt(5.0), 1.0])
    derivative = np.zeros((4, 4))
    for target in range(4):
        for source in range(4):
            if target != source:
                weight_target = np.prod(
                    [points[target] - points[middle] for middle in range(4) if middle != target]
                )
                weight_source = np.prod(
                    [points[source] - points[middle] for middle in range(4) if middle != source]
                )
                derivative[target, source] = weight_target / (
                    weight_source * (points[target] - points[source])
                )
        derivative[target, target] = np.sum(
            [1.0 / (points[target] - points[middle]) for middle in range(4) if middle != target]
        )
    return derivative


def node_weights():
    derivative = lobatto_derivative()
    along_first = np.kron(np.eye(4), derivative)
    along_second = np.kron(derivative, np.eye(4))
    laplace = along_first @ along_first + along_second @ along_second
    edges = np.zeros((4, 4))
    edges[0, :] += 1.0
    edges[3, :] += 1.0
    edges[:, 0] += 1.0
    edges[:, 3] += 1.0
    linear = VISCOSITY * laplace - PENALTY * np.diag(edges.reshape(-1))
    repeat = np.eye(LANES // NODES)
    return np.concatenate(
        [np.kron(repeat, linear.T), np.kron(repeat, -DRIFT * along_first.T)], axis=1
    ).astype(np.float32)


def each(count, body):
    if count <= 16:
        for index in range(count):
            body(index)
    else:
        lax.fori_loop(0, count, lambda index, carry: (body(index), carry)[1], 0)


def lane_ids(rows=ROWS):
    return lax.broadcasted_iota(jnp.int32, (rows, LANES), 1)


def row_ids():
    return lax.broadcasted_iota(jnp.int32, (ROWS, LANES), 0)


def pick(values, lanes):
    return jnp.take_along_axis(values, lanes, axis=1, mode="promise_in_bounds")


def half_turn(values):
    return pltpu.roll(values, LANES // 2, 1)


def split_pair(first, second):
    lower = lane_ids() < LANES // 2
    return (
        jnp.where(lower, first, half_turn(second)),
        jnp.where(lower, half_turn(first), second),
    )


def row_of(values, row):
    return jnp.broadcast_to(values[row : row + 1], (ROWS, LANES))


def pack_kernel(
    nbr_hbm,
    face_hbm,
    order_hbm,
    state_hbm,
    weight_hbm,
    out_ref,
    weight_ref,
    nbr_ref,
    face_ref,
    order_ref,
    state_ref,
    scratch,
    sems,
    depth,
    block,
):
    copies = [
        pltpu.make_async_copy(source, target, sems.at[n])
        for n, (source, target) in enumerate(
            (
                (nbr_hbm, nbr_ref),
                (face_hbm, face_ref),
                (order_hbm, order_ref),
                (state_hbm, state_ref),
                (weight_hbm, weight_ref),
            )
        )
    ]
    for copy in copies:
        copy.start()
    elements, variables, nodes, levels = state_ref.shape
    used = levels // depth
    half = LANES // 2
    lane = lane_ids()
    own = lax.axis_index("vars")
    column = lane % half
    elem = column // nodes
    along_y = (column // 4) % 4
    along_x = column % 4
    upper = lane >= half
    edge = jnp.where(
        upper,
        jnp.where(along_x == 3, 1, jnp.where(along_x == 0, 3, -1)),
        jnp.where(along_y == 0, 0, jnp.where(along_y == 3, 2, -1)),
    )
    along = jnp.where(upper, along_y, along_x)
    place = jnp.where(edge >= 2, 3 - along, along)
    out_ref[...] = jnp.zeros_like(out_ref)
    copies[0].wait()
    copies[1].wait()
    far = jnp.zeros_like(lane)
    face = jnp.zeros_like(lane)
    for e in range(elements):
        for j in range(4):
            here = (elem == e) & (edge == j)
            far = jnp.where(here, nbr_ref[e, j], far)
            face = jnp.where(here, face_ref[e, j], face)
    node = jnp.where(
        face == 0,
        3 - place,
        jnp.where(face == 1, 15 - 4 * place, jnp.where(face == 2, 12 + place, 4 * place)),
    )
    far_col = jnp.where(edge >= 0, nodes * far + node, -1).astype(jnp.float32)

    copies[2].wait()
    order = order_ref[...]
    spots = lax.broadcasted_iota(jnp.int32, (block, block), 0)
    marks = (spots == order).astype(jnp.float32).astype(jnp.bfloat16)
    numbers = lax.broadcasted_iota(jnp.int32, (ROWS, block), 1).astype(jnp.float32)
    scratch[0] = jnp.broadcast_to(order, (ROWS, block)).astype(jnp.float32)
    scratch[1] = lax.dot_general(
        numbers.astype(jnp.bfloat16),
        marks,
        (((1,), (1,)), ((), ())),
        preferred_element_type=jnp.float32,
    )
    begin = pl.multiple_of((own // 2) * LANES, LANES)
    order_part = scratch[0, :, pl.ds(begin, LANES)]
    place_part = scratch[1, :, pl.ds(begin, LANES)]
    odd = own % 2 == 1
    order_part = jnp.where(odd, half_turn(order_part), order_part)
    place_part = jnp.where(odd, place_part, half_turn(place_part))
    indices = jnp.where(upper, place_part, order_part)

    slots = out_ref.shape[0] // ROWS
    for first in range(0, slots, ROWS):
        out_ref[pl.ds(ROWS * first + FAR_ROW, ROWS, stride=ROWS), :] = far_col
        out_ref[pl.ds(ROWS * first + ORDER_ROW, ROWS, stride=ROWS), :] = indices
    copies[3].wait()
    for pair in range(variables // 2):
        fields = jnp.concatenate(
            [
                state_ref[:, pair].reshape(elements * nodes, levels),
                state_ref[:, variables // 2 + pair].reshape(elements * nodes, levels),
            ],
            axis=0,
        )
        by_level = fields.T
        for part in range(depth):
            for first in range(0, used, ROWS):
                begin = used * part + first
                out_ref[pl.ds(ROWS * first + depth * pair + part, ROWS, stride=ROWS), :] = (
                    by_level[begin : begin + ROWS]
                )
    copies[4].wait()


def tendency_kernel(got_ref, weight_ref, out_ref, partial_ref, field, linear, tend, depth, share):
    tiles = field.shape[0]
    block = LANES * 2
    tiles_block = block // LANES
    col_count = block // share
    lane = lane_ids()
    row = row_ids()
    lower = lane < LANES // 2

    def unpack(q):
        low, high = split_pair(got_ref[2 * q], got_ref[2 * q + 1])
        field[q, 0] = low
        field[q, 1] = high

    each(tiles, unpack)

    step = min(tiles, 16)

    def multiply(chunk):
        fields = field[pl.ds(chunk * step, step)].reshape(step * 2 * ROWS, LANES)
        result = jnp.dot(fields, weight_ref[...], precision=EXACT)
        linear[pl.ds(chunk * step, step)] = result.reshape(step, 2, ROWS, 2 * LANES)

    each(tiles // step, multiply)

    def advance(q):
        before = (q + tiles - 1) % tiles
        after = (q + 1) % tiles
        high = field[q, 1]
        wind = jnp.where(row < depth, pltpu.roll(high, ROWS - depth, 0), high)
        sums = [jnp.zeros((ROWS, LANES), jnp.float32)] * 2
        for side in range(2):
            far = row_of(field[q, side], FAR_ROW).astype(jnp.int32)
            spot = jnp.maximum(far, 0) % LANES
            inside = far // LANES == q
            for part in range(2):
                beside = jnp.where(lower, field[after, part], field[before, part])
                value = jnp.where(inside, pick(field[q, part], spot), pick(beside, spot))
                sums[part] = sums[part] + jnp.where(far >= 0, value, 0.0)
        for part in range(2):
            own = field[q, part]
            result = (
                linear[q, part, :, :LANES]
                + wind * linear[q, part, :, LANES:]
                + PENALTY * sums[part]
            )
            tend[q, part] = result
            partial_ref[q, part] = jnp.where(row < FAR_ROW, own + TIME_STEP * result, own)

    each(tiles, advance)

    def arrange(p):
        col = p // tiles_block
        order = row_of(field[p, 0], ORDER_ROW).astype(jnp.int32)
        owner = order // share
        spot = (share * col) % LANES + order % share
        base = (share * col) // LANES
        parts = [jnp.zeros((ROWS, LANES), jnp.float32)] * 2
        for k in range(col_count):
            for part in range(2):
                source = tend[tiles_block * k + base, part]
                parts[part] = jnp.where(owner == k, pick(source, spot), parts[part])
        first, second = split_pair(parts[0], parts[1])
        out_ref[2 * p] = first
        out_ref[2 * p + 1] = second

    each(tiles, arrange)


def in_two(values):
    high = values.astype(jnp.bfloat16)
    low = (values - high.astype(jnp.float32)).astype(jnp.bfloat16)
    return high, low


def pool_weights(step, wide):
    lane = lax.broadcasted_iota(jnp.int32, (wide, LANES), 1) % (LANES // 2)
    owner = lax.broadcasted_iota(jnp.int32, (wide, LANES), 0) // CCOL
    mean = 1.0 / (CCOL * TIME_STEP)
    return jnp.where(lane == (wide // CCOL) * step + owner, mean, 0.0).astype(jnp.bfloat16)


def pooled_sum(tiles, step):
    rows = ROWS * len(tiles[0])
    joined = jnp.concatenate([jnp.concatenate(tile, axis=0) for tile in tiles], axis=1)
    high, low = in_two(joined)
    both = jnp.concatenate([high, low], axis=0)
    weights = pool_weights(step, LANES * len(tiles))
    result = jnp.dot(both, weights, preferred_element_type=jnp.float32)
    return result[:rows] + result[rows:]


def settle_kernel(
    cloud_hbm, down_hbm, up_hbm, base_ref, mean_ref, down_ref, up_ref, cloud_ref, sems, wide
):
    clev, variables, width = cloud_ref.shape
    steps = width // (LANES * wide)
    span = LANES * wide
    small = [
        pltpu.make_async_copy(down_hbm, down_ref, sems.at[steps]),
        pltpu.make_async_copy(up_hbm, up_ref, sems.at[steps + 1]),
    ]

    def fetch(n):
        here = pl.ds(pl.multiple_of(n * span, span), span)
        return pltpu.make_async_copy(
            cloud_hbm.at[:, :, here], cloud_ref.at[:, :, here], sems.at[n]
        )

    for n in range(steps):
        fetch(n).start()
    for copy in small:
        copy.start()
    mean_ref[...] = jnp.zeros_like(mean_ref)
    lane = lane_ids()
    row = row_ids()
    within = lane % CCOL
    wind_row = (row // variables) * variables + 3
    first_half = row < variables
    pairs = clev // 2
    zero = jnp.zeros((ROWS, LANES), jnp.float32)

    def tile(begin):
        def load(a):
            return cloud_ref[2 * a : 2 * a + 2, :, pl.ds(begin, LANES)].reshape(ROWS, LANES)

        turned_before = zero
        now = load(0)
        turned = pltpu.roll(now, variables, 0)
        seen = []
        for a in range(pairs):
            following = load(a + 1) if a + 1 < pairs else zero
            turned_after = pltpu.roll(following, variables, 0) if a + 1 < pairs else zero
            above = jnp.where(first_half, turned, turned_after)
            below = jnp.where(first_half, turned_before, turned)
            ahead = jnp.where(
                within == CCOL - 1, pltpu.roll(now, CCOL - 1, 1), pltpu.roll(now, LANES - 1, 1)
            )
            behind = jnp.where(
                within == 0, pltpu.roll(now, LANES - CCOL + 1, 1), pltpu.roll(now, 1, 1)
            )
            wind = jnp.take_along_axis(now, wind_row, axis=0, mode="promise_in_bounds")
            advect = (-CLOUD_ADVECT * TIME_STEP) * wind * (ahead - behind)
            diffuse = (CLOUD_DIFFUSE * TIME_STEP) * (above - 2.0 * now + below)
            base_ref[ROWS * a : ROWS * a + ROWS, pl.ds(begin, LANES)] = now + (advect + diffuse)
            seen.append(now)
            turned_before, turned, now = turned, turned_after, following
        return seen

    def advance(step, carry):
        fetch(step).wait()
        tiles = [tile(pl.multiple_of(step * span + LANES * n, LANES)) for n in range(wide)]
        mean_ref[...] += pooled_sum(tiles, step)
        return carry

    lax.fori_loop(0, steps, advance, 0)
    for copy in small:
        copy.wait()


def cloud_kernel(
    got_ref,
    base_ref,
    mean_ref,
    down_ref,
    up_ref,
    next_hbm,
    out_ref,
    forced,
    pooled,
    next_ref,
    sem,
    depth,
    levels,
    wide,
):
    clev, variables, width = next_ref.shape
    steps = width // (LANES * wide)
    span = LANES * wide
    used = levels // depth
    lane = lane_ids()
    row = row_ids()
    half = LANES // 2
    fields = jnp.concatenate(
        [
            jnp.concatenate(
                [
                    got_ref[pl.ds(ROWS * first + depth * pair + part, ROWS, stride=ROWS), :]
                    for part in range(depth)
                    for first in range(0, used, ROWS)
                ],
                axis=0,
            )
            for pair in range(2)
        ],
        axis=1,
    )
    forcing = TIME_STEP * jnp.dot(down_ref[...], fields, precision=EXACT)
    for pair in range(2):
        straight = forcing[:, LANES * pair : LANES * pair + LANES]
        turned = half_turn(straight)
        for first in range(0, clev, ROWS):
            count = min(ROWS, clev - first)
            for shift, values in ((0, straight), (2, turned)):
                forced[
                    pl.ds(variables * first + shift + pair, count, stride=variables), :
                ] = values[first : first + count]
    pooled[...] = -mean_ref[...]
    var = row % variables
    lead_row = (row // variables) * variables
    keep = jnp.where(var == 2, RETAIN, 1.0).astype(jnp.float32)
    sign = jnp.where(var == 1, -1.0, jnp.where(var == 3, 0.0, 1.0)).astype(jnp.float32)
    sign = CONDENSE_RATE * sign
    pairs = clev // 2

    def tile(begin, index):
        spread = (LANES // CCOL) * index + lane // CCOL
        results = []
        for a in range(pairs):
            push = pick(forced[ROWS * a : ROWS * a + ROWS, :], spread)
            moved = base_ref[ROWS * a : ROWS * a + ROWS, pl.ds(begin, LANES)] + push
            excess = pltpu.roll(moved, ROWS - 1, 0) - SATURATION_BASE * jnp.exp(
                SATURATION_SLOPE * moved
            )
            soft = jnp.maximum(excess, 0.0) + jnp.log(1.0 + jnp.exp(-jnp.abs(excess)))
            condensed = jnp.take_along_axis(soft, lead_row, axis=0, mode="promise_in_bounds")
            updated = keep * moved + sign * condensed
            next_ref[2 * a : 2 * a + 2, :, pl.ds(begin, LANES)] = updated.reshape(
                2, variables, LANES
            )
            results.append(updated)
        return results

    def store(step):
        here = pl.ds(pl.multiple_of(step * span, span), span)
        return pltpu.make_async_copy(next_ref.at[:, :, here], next_hbm.at[:, :, here], sem)

    def advance(step, carry):
        tiles = [
            tile(pl.multiple_of(step * span + LANES * n, LANES), wide * step + n)
            for n in range(wide)
        ]
        store(step).start()
        pooled[...] += pooled_sum(tiles, step)
        return carry

    lax.fori_loop(0, steps, advance, 0)
    lower = lane_ids(clev) < half
    mean = jnp.concatenate(
        [
            jnp.where(
                lower,
                pooled[pl.ds(pair, clev, stride=variables), :],
                pooled[pl.ds(2 + pair, clev, stride=variables), :],
            )
            for pair in range(2)
        ],
        axis=1,
    )
    feedback = lax.dot_general(up_ref[...], mean, (((0,), (0,)), ((), ())), precision=EXACT)
    for pair in range(2):
        for part in range(depth):
            for first in range(0, used, ROWS):
                begin = used * part + first
                out_ref[pl.ds(ROWS * first + depth * pair + part, ROWS, stride=ROWS), :] = (
                    feedback[begin : begin + ROWS, LANES * pair : LANES * pair + LANES]
                )
    pltpu.make_async_copy(next_ref, next_hbm, sem).wait()


def update_kernel(got_ref, partial_ref, out_ref, field, share):
    tiles = field.shape[0]
    block = LANES * 2
    tiles_block = block // LANES
    lane = lane_ids()
    groups = LANES // share
    group = lane // share
    inner = lane % share

    def unpack(p):
        low, high = split_pair(got_ref[2 * p], got_ref[2 * p + 1])
        field[p, 0] = low
        field[p, 1] = high

    each(tiles, unpack)

    def collect(q):
        k = q // tiles_block
        start = (LANES * (q % tiles_block)) // share
        offset = share * k
        place = jnp.zeros((ROWS, LANES), jnp.float32)
        for g in range(groups):
            source = row_of(partial_ref[tiles_block * (start + g) + offset // LANES, 1], ORDER_ROW)
            place = jnp.where(group == g, pick(source, offset % LANES + inner), place)
        place = place.astype(jnp.int32)
        spot = place % LANES
        parts = [jnp.zeros((ROWS, LANES), jnp.float32)] * 2
        for g in range(groups):
            for piece in range(tiles_block):
                chosen = (group == g) & (place // LANES == piece)
                for part in range(2):
                    source = field[tiles_block * (start + g) + piece, part]
                    parts[part] = jnp.where(chosen, pick(source, spot), parts[part])
        low = partial_ref[q, 0] + TIME_STEP * parts[0]
        high = partial_ref[q, 1] + TIME_STEP * parts[1]
        first, second = split_pair(low, high)
        out_ref[2 * q] = first
        out_ref[2 * q + 1] = second

    each(tiles, collect)


def unpack_kernel(got_ref, state_ref, depth):
    elements, variables, nodes, levels = state_ref.shape
    used = levels // depth
    for pair in range(variables // 2):
        by_level = jnp.concatenate(
            [
                got_ref[pl.ds(ROWS * first + depth * pair + part, ROWS, stride=ROWS), :]
                for part in range(depth)
                for first in range(0, used, ROWS)
            ],
            axis=0,
        )
        fields = by_level.T.reshape(2, elements, nodes, levels)
        state_ref[:, pair] = fields[0]
        state_ref[:, variables // 2 + pair] = fields[1]


def kernel_call(body, name, results, scratch, *operands, hbm_in=(), hbm_out=(), cost=None):
    spec = {True: pl.BlockSpec(memory_space=pltpu.HBM), False: pl.BlockSpec(memory_space=pltpu.VMEM)}
    operands = [
        pltpu.with_memory_space_constraint(value, pltpu.HBM) if n in hbm_in else value
        for n, value in enumerate(operands)
    ]
    return pl.pallas_call(
        body,
        name=name,
        out_shape=results,
        in_specs=[spec[n in hbm_in] for n in range(len(operands))],
        out_specs=tuple(spec[n in hbm_out] for n in range(len(results))),
        scratch_shapes=scratch,
        cost_estimate=cost,
        compiler_params=pltpu.CompilerParams(vmem_limit_bytes=KERNEL_VMEM),
    )(*operands)


def exchange(slots):
    return lax.all_to_all(slots, AXES, split_axis=0, concat_axis=0, tiled=True)


def shards(
    model_state,
    cloud_state,
    neighbor,
    facing_edge,
    column_order,
    model_to_cloud_levels,
    cloud_to_model_levels,
):
    elements, variables, nodes, levels = model_state.shape
    clev, width = cloud_state.shape[1:]
    devices = lax.axis_size(AXES)
    block = column_order.shape[1]
    share = block // lax.axis_size("cols")
    depth = -(-levels // devices)
    assert variables == 4 and nodes == NODES and 2 * elements * nodes == LANES
    assert 2 * depth <= FAR_ROW and levels % (ROWS * depth) == 0 and block == 2 * LANES
    tiles = devices // 2
    f32 = jnp.float32
    shape = jax.ShapeDtypeStruct
    flat = shape((devices * ROWS, LANES), f32)
    slots = shape((devices, ROWS, LANES), f32)
    pairs = shape((tiles, 2, ROWS, LANES), f32)
    columns = width // LANES
    wide = 2 if columns % 2 == 0 else 1
    dma = pltpu.SemaphoreType.DMA

    packed, weights = kernel_call(
        functools.partial(pack_kernel, depth=depth, block=block),
        "pack_state",
        (flat, shape((LANES, 2 * LANES), f32)),
        [
            pltpu.SMEM(neighbor.shape, jnp.int32),
            pltpu.SMEM(facing_edge.shape, jnp.int32),
            pltpu.VMEM(column_order.shape, jnp.int32),
            pltpu.VMEM(model_state.shape, f32),
            pltpu.VMEM((2, ROWS, block), f32),
            dma((5,)),
        ],
        neighbor,
        facing_edge,
        column_order,
        model_state,
        jnp.asarray(node_weights()),
        hbm_in=range(5),
    )
    by_level = exchange(packed.reshape(slots.shape))
    arranged, partial = kernel_call(
        functools.partial(tendency_kernel, depth=depth, share=share),
        "tendency",
        (slots, pairs),
        [
            pltpu.VMEM(pairs.shape, f32),
            pltpu.VMEM((tiles, 2, ROWS, 2 * LANES), f32),
            pltpu.VMEM(pairs.shape, f32),
        ],
        by_level,
        weights,
    )
    base, mean, down, up = kernel_call(
        functools.partial(settle_kernel, wide=wide),
        "settle",
        (
            shape((clev * variables, width), f32),
            shape((clev * variables, LANES), f32),
            shape((clev, levels), f32),
            shape((clev, levels), f32),
        ),
        [pltpu.VMEM((clev, variables, width), f32), dma((columns // wide + 2,))],
        jnp.transpose(cloud_state, (1, 0, 2)),
        model_to_cloud_levels,
        cloud_to_model_levels.T,
        hbm_in=range(3),
        cost=pl.CostEstimate(flops=10**8, bytes_accessed=4 * 10**6, transcendentals=0),
    )
    by_column = exchange(arranged)
    cloud_next, fed = kernel_call(
        functools.partial(cloud_kernel, depth=depth, levels=levels, wide=wide),
        "cloud",
        (shape((clev, variables, width), f32), flat),
        [
            pltpu.VMEM((clev * variables, LANES), f32),
            pltpu.VMEM((clev * variables, LANES), f32),
            pltpu.VMEM((clev, variables, width), f32),
            dma,
        ],
        by_column.reshape(flat.shape),
        base,
        mean,
        down,
        up,
        hbm_out=(0,),
    )
    fed_level = exchange(fed.reshape(slots.shape))
    (advanced,) = kernel_call(
        functools.partial(update_kernel, share=share),
        "update",
        (slots,),
        [pltpu.VMEM(pairs.shape, f32)],
        fed_level,
        partial,
    )
    home = exchange(advanced)
    (model_next,) = kernel_call(
        functools.partial(unpack_kernel, depth=depth),
        "unpack_state",
        (shape(model_state.shape, f32),),
        [],
        home.reshape(flat.shape),
    )
    return (model_next, jnp.transpose(cloud_next, (1, 0, 2)))


def solution(mesh):
    placed = (
        P(AXES, None, None, None),
        P(None, None, AXES),
        P(AXES, None),
        P(AXES, None),
        P("cols", None),
        P(),
        P(),
    )
    return jax.shard_map(
        shards,
        mesh=mesh,
        in_specs=placed,
        out_specs=(P(AXES, None, None, None), P(None, None, AXES)),
        check_vma=False,
    )
```

```python
import functools

import jax
import jax.numpy as jnp
import numpy as np
from jax import lax
from jax.experimental import pallas as pl
from jax.experimental.pallas import tpu as pltpu
from jax.sharding import PartitionSpec as P

CCOL = 32
NODES = 16
LANES = 128
ROWS = 8
AXES = ("cols", "vars")
VISCOSITY = 0.01
DRIFT = 0.05
PENALTY = 0.5
TIME_STEP = 0.5
CLOUD_ADVECT = 0.25
CLOUD_DIFFUSE = 0.1
CONDENSE_RATE = 0.3
SATURATION_BASE = 0.5
SATURATION_SLOPE = 0.3
RETAIN = 0.8
EXACT = lax.Precision.HIGHEST
KERNEL_VMEM = 16 * 2**20
WIDE = 2
GROUP = 16
SWAPS = 4
FAR_ROW = 6
ORDER_ROW = 7


def lobatto_derivative():
    points = np.array([-1.0, -1.0 / np.sqrt(5.0), 1.0 / np.sqrt(5.0), 1.0])
    derivative = np.zeros((4, 4))
    for target in range(4):
        for source in range(4):
            if target != source:
                weight_target = np.prod(
                    [points[target] - points[middle] for middle in range(4) if middle != target]
                )
                weight_source = np.prod(
                    [points[source] - points[middle] for middle in range(4) if middle != source]
                )
                derivative[target, source] = weight_target / (
                    weight_source * (points[target] - points[source])
                )
        derivative[target, target] = np.sum(
            [1.0 / (points[target] - points[middle]) for middle in range(4) if middle != target]
        )
    return derivative


def node_weights():
    derivative = lobatto_derivative()
    along_first = np.kron(np.eye(4), derivative)
    along_second = np.kron(derivative, np.eye(4))
    laplace = along_first @ along_first + along_second @ along_second
    edges = np.zeros((4, 4))
    edges[0, :] += 1.0
    edges[3, :] += 1.0
    edges[:, 0] += 1.0
    edges[:, 3] += 1.0
    linear = VISCOSITY * laplace - PENALTY * np.diag(edges.reshape(-1))
    repeat = np.eye(LANES // NODES)
    weights = np.concatenate(
        [np.kron(repeat, linear.T), np.kron(repeat, -DRIFT * along_first.T)], axis=1
    )
    high = weights.astype(jnp.bfloat16)
    low = (weights - high.astype(np.float64)).astype(jnp.bfloat16)
    return jnp.asarray(np.stack([high, low]))


def each(count, body, group=GROUP):
    group = min(group, count)
    if count <= group:
        for index in range(count):
            body(index)
        return

    def several(first, carry):
        for n in range(group):
            body(first * group + n)
        return carry

    lax.fori_loop(0, count // group, several, 0)


def lane_ids(rows=ROWS):
    return lax.broadcasted_iota(jnp.int32, (rows, LANES), 1)


def row_ids():
    return lax.broadcasted_iota(jnp.int32, (ROWS, LANES), 0)


def pick(values, lanes):
    return jnp.take_along_axis(values, lanes, axis=1, mode="promise_in_bounds")


def half_turn(values):
    return pltpu.roll(values, LANES // 2, 1)


def split_pair(first, second):
    lower = lane_ids() < LANES // 2
    return (
        jnp.where(lower, first, half_turn(second)),
        jnp.where(lower, half_turn(first), second),
    )


def row_of(values, row):
    return jnp.broadcast_to(values[row : row + 1], (ROWS, LANES))


def unpack_pairs(got_ref, field):
    def unpack(q):
        low, high = split_pair(got_ref[2 * q], got_ref[2 * q + 1])
        field[q, 0] = low
        field[q, 1] = high

    each(field.shape[0], unpack)


def pack_pair(out_ref, q, low, high):
    first, second = split_pair(low, high)
    out_ref[2 * q] = first
    out_ref[2 * q + 1] = second


def swap_groups(source, target, share):
    groups = LANES // share
    group = lane_ids() // share

    def swap(index):
        x = index // 2
        y = index % 2

        def gather(w):
            for part in range(2):
                joined = source[2 * groups * x + y, part]
                joined = pltpu.roll(joined, (LANES - share * w) % LANES, 1)
                for u in range(1, groups):
                    other = source[2 * (groups * x + u) + y, part]
                    turned = pltpu.roll(other, (share * (u + groups - w)) % LANES, 1)
                    joined = jnp.where(group == u, turned, joined)
                target[2 * (groups * y + w) + x, part] = joined

        each(groups, gather)

    each(4, swap, SWAPS)


def reorder(source, block_tile, places):
    spot = places & (LANES - 1)
    first = places < LANES
    return [
        jnp.where(
            first,
            pick(source[block_tile, part], spot),
            pick(source[block_tile + 1, part], spot),
        )
        for part in range(2)
    ]


def pack_kernel(
    nbr_hbm,
    face_hbm,
    order_hbm,
    state_hbm,
    weight_hbm,
    out_ref,
    weight_ref,
    nbr_ref,
    face_ref,
    order_ref,
    state_ref,
    scratch,
    sems,
    depth,
    block,
):
    copies = [
        pltpu.make_async_copy(source, target, sems.at[n])
        for n, (source, target) in enumerate(
            (
                (nbr_hbm, nbr_ref),
                (face_hbm, face_ref),
                (order_hbm, order_ref),
                (state_hbm, state_ref),
                (weight_hbm, weight_ref),
            )
        )
    ]
    for copy in copies:
        copy.start()
    elements, variables, nodes, levels = state_ref.shape
    used = levels // depth
    half = LANES // 2
    lane = lane_ids()
    own = lax.axis_index("vars")
    column = lane % half
    elem = column // nodes
    along_y = (column // 4) % 4
    along_x = column % 4
    upper = lane >= half
    edge = jnp.where(
        upper,
        jnp.where(along_x == 3, 1, jnp.where(along_x == 0, 3, -1)),
        jnp.where(along_y == 0, 0, jnp.where(along_y == 3, 2, -1)),
    )
    along = jnp.where(upper, along_y, along_x)
    place = jnp.where(edge >= 2, 3 - along, along)
    out_ref[...] = jnp.zeros_like(out_ref)
    copies[0].wait()
    copies[1].wait()
    far = jnp.zeros_like(lane)
    face = jnp.zeros_like(lane)
    for e in range(elements):
        for j in range(4):
            here = (elem == e) & (edge == j)
            far = jnp.where(here, nbr_ref[e, j], far)
            face = jnp.where(here, face_ref[e, j], face)
    node = jnp.where(
        face == 0,
        3 - place,
        jnp.where(face == 1, 15 - 4 * place, jnp.where(face == 2, 12 + place, 4 * place)),
    )
    far_col = jnp.where(edge >= 0, nodes * far + node, -1).astype(jnp.float32)

    copies[2].wait()
    order = order_ref[...]
    spots = lax.broadcasted_iota(jnp.int32, (block, block), 0)
    marks = (spots == order).astype(jnp.float32).astype(jnp.bfloat16)
    numbers = lax.broadcasted_iota(jnp.int32, (ROWS, block), 1).astype(jnp.float32)
    scratch[0] = jnp.broadcast_to(order, (ROWS, block)).astype(jnp.float32)
    scratch[1] = lax.dot_general(
        numbers.astype(jnp.bfloat16),
        marks,
        (((1,), (1,)), ((), ())),
        preferred_element_type=jnp.float32,
    )
    begin = pl.multiple_of((own // 2) * LANES, LANES)
    order_part = scratch[0, :, pl.ds(begin, LANES)]
    place_part = scratch[1, :, pl.ds(begin, LANES)]
    odd = own % 2 == 1
    order_part = jnp.where(odd, half_turn(order_part), order_part)
    place_part = jnp.where(odd, place_part, half_turn(place_part))
    indices = jnp.where(upper, place_part, order_part)

    slots = out_ref.shape[0] // ROWS
    for first in range(0, slots, ROWS):
        out_ref[pl.ds(ROWS * first + FAR_ROW, ROWS, stride=ROWS), :] = far_col
        out_ref[pl.ds(ROWS * first + ORDER_ROW, ROWS, stride=ROWS), :] = indices
    copies[3].wait()
    for pair in range(variables // 2):
        fields = jnp.concatenate(
            [
                state_ref[:, pair].reshape(elements * nodes, levels),
                state_ref[:, variables // 2 + pair].reshape(elements * nodes, levels),
            ],
            axis=0,
        )
        by_level = fields.T
        for part in range(depth):
            for first in range(0, used, ROWS):
                begin = used * part + first
                out_ref[pl.ds(ROWS * first + depth * pair + part, ROWS, stride=ROWS), :] = (
                    by_level[begin : begin + ROWS]
                )
    copies[4].wait()


def tendency_kernel(
    got_ref, weight_ref, out_ref, partial_ref, field, linear, tend, moved, depth, share
):
    tiles = field.shape[0]
    row = row_ids()
    lower = lane_ids() < LANES // 2
    unpack_pairs(got_ref, field)
    step = min(tiles, 16)

    def multiply(chunk):
        fields = field[pl.ds(chunk * step, step)].reshape(step * 2 * ROWS, LANES)
        high, low = in_two(fields)
        coarse, fine = weight_ref[0], weight_ref[1]
        result = jnp.dot(
            jnp.concatenate([high, low], axis=1),
            jnp.concatenate([coarse, coarse], axis=0),
            preferred_element_type=jnp.float32,
        ) + jnp.dot(high, fine, preferred_element_type=jnp.float32)
        linear[pl.ds(chunk * step, step)] = result.reshape(step, 2, ROWS, 2 * LANES)

    each(tiles // step, multiply, 1)

    def advance(q):
        before = jnp.where(q == 0, tiles - 1, q - 1)
        after = jnp.where(q == tiles - 1, 0, q + 1)
        high = field[q, 1]
        wind = jnp.where(row < depth, pltpu.roll(high, ROWS - depth, 0), high)
        sums = [0.0, 0.0]
        for side in range(2):
            far = row_of(field[q, side], FAR_ROW).astype(jnp.int32)
            spot = far & (LANES - 1)
            inside = lax.shift_right_arithmetic(far, 7) == q
            for part in range(2):
                beside = jnp.where(lower, field[after, part], field[before, part])
                value = jnp.where(inside, pick(field[q, part], spot), pick(beside, spot))
                sums[part] = sums[part] + jnp.where(far >= 0, value, 0.0)
        for part in range(2):
            own = field[q, part]
            result = (
                linear[q, part, :, :LANES]
                + wind * linear[q, part, :, LANES:]
                + PENALTY * sums[part]
            )
            tend[q, part] = result
            partial_ref[q, part] = jnp.where(row < FAR_ROW, own + TIME_STEP * result, own)

    each(tiles, advance)
    swap_groups(tend, moved, share)

    def arrange(p):
        order = row_of(field[p, 0], ORDER_ROW).astype(jnp.int32)
        pack_pair(out_ref, p, *reorder(moved, p // 2 * 2, order))

    each(tiles, arrange)


def in_two(values):
    high = values.astype(jnp.bfloat16)
    low = (values - high.astype(jnp.float32)).astype(jnp.bfloat16)
    return high, low


def pool_weights(step):
    wide = WIDE * LANES
    lane = lax.broadcasted_iota(jnp.int32, (wide, LANES), 1) % (LANES // 2)
    owner = lax.broadcasted_iota(jnp.int32, (wide, LANES), 0) // CCOL
    mean = 1.0 / (CCOL * TIME_STEP)
    return jnp.where(lane == (wide // CCOL) * step + owner, mean, 0.0).astype(jnp.bfloat16)


def pooled_sum(tiles, weights):
    joined = jnp.concatenate([jnp.concatenate(tile, axis=0) for tile in tiles], axis=1)
    rows = joined.shape[0]
    both = jnp.concatenate(in_two(joined), axis=0)
    result = jnp.dot(both, weights, preferred_element_type=jnp.float32)
    return result[:rows] + result[rows:]


def settle_kernel(
    cloud_hbm,
    down_hbm,
    up_hbm,
    base_ref,
    mean_ref,
    pool_ref,
    down_ref,
    up_ref,
    cloud_ref,
    sums,
    sems,
):
    columns, variables, deep = base_ref.shape[:3]
    clev = cloud_hbm.shape[0]
    plane = (columns + 1) * variables
    steps = columns // WIDE
    small = [
        pltpu.make_async_copy(down_hbm, down_ref, sems.at[steps]),
        pltpu.make_async_copy(up_hbm, up_ref, sems.at[steps + 1]),
    ]

    def fetch(step):
        here = pl.ds(WIDE * step, WIDE)
        return pltpu.make_async_copy(
            cloud_hbm.at[:, here], cloud_ref.at[pl.ds(1, clev), here], sems.at[step]
        )

    for step in range(steps):
        fetch(step).start()
    for copy in small:
        copy.start()
    flat_ref = cloud_ref.reshape((deep + 2) * plane, LANES)
    rim = jnp.zeros((plane, LANES), jnp.float32)
    flat_ref[0:plane] = rim
    for level in range(clev, deep + 1):
        flat_ref[(level + 1) * plane : (level + 2) * plane] = rim
    sums[...] = jnp.zeros_like(sums)
    within = lane_ids() % CCOL
    last = within == CCOL - 1
    first = within == 0

    def tile(t):
        def load(level, variable):
            begin = (level + 1) * plane + variables * t + variable
            return flat_ref[pl.ds(begin, ROWS, stride=plane), :]

        changes = []
        winds = [
            (-CLOUD_ADVECT * TIME_STEP) * load(level, 3) for level in range(0, deep, ROWS)
        ]
        for variable in range(variables):
            for level in range(0, deep, ROWS):
                now = load(level, variable)
                ahead = jnp.where(
                    last, pltpu.roll(now, CCOL - 1, 1), pltpu.roll(now, LANES - 1, 1)
                )
                behind = jnp.where(
                    first, pltpu.roll(now, LANES - CCOL + 1, 1), pltpu.roll(now, 1, 1)
                )
                around = load(level - 1, variable) + load(level + 1, variable)
                change = winds[level // ROWS] * (ahead - behind) + (
                    CLOUD_DIFFUSE * TIME_STEP
                ) * (around - 2.0 * now)
                base = now + change
                base_ref[t, variable, level : level + ROWS, :] = base
                changes.append(RETAIN * base - now if variable == 2 else change)
        return changes

    def advance(step, carry):
        fetch(step).wait()
        weights = pool_weights(step)
        pool_ref[step] = weights
        sums[...] += pooled_sum([tile(WIDE * step + n) for n in range(WIDE)], weights)
        return carry

    lax.fori_loop(0, steps, advance, 0)
    lower = lane_ids(deep) < LANES // 2
    for pair in range(2):
        mean_ref[pair] = jnp.where(
            lower,
            sums[deep * pair : deep * (pair + 1)],
            sums[deep * (2 + pair) : deep * (3 + pair)],
        )
    for copy in small:
        copy.wait()


def cloud_kernel(
    got_ref,
    base_ref,
    mean_ref,
    pool_ref,
    down_ref,
    up_ref,
    next_hbm,
    out_ref,
    forced,
    sums,
    next_ref,
    sem,
    depth,
):
    columns, variables, deep = base_ref.shape[:3]
    clev, levels = down_ref.shape
    plane = (columns + 1) * variables
    flat_ref = next_ref.reshape(clev * plane, LANES)
    steps = columns // WIDE
    used = levels // depth
    half = LANES // 2
    fields = jnp.concatenate(
        [
            jnp.concatenate(
                [
                    got_ref[pl.ds(ROWS * first + depth * pair + part, ROWS, stride=ROWS), :]
                    for part in range(depth)
                    for first in range(0, used, ROWS)
                ],
                axis=0,
            )
            for pair in range(2)
        ],
        axis=1,
    )
    forcing = jnp.dot(TIME_STEP * down_ref[...], fields, precision=EXACT)
    for pair in range(2):
        forced[pair, 0:clev] = forcing[:, LANES * pair : LANES * pair + LANES]
        forced[pair, clev:deep] = jnp.zeros((deep - clev, LANES), jnp.float32)
    sums[...] = jnp.zeros_like(sums)
    owner = lane_ids() // CCOL

    def tile(t):
        near = (LANES // CCOL) * t + owner
        spots = (near, near, near + half, near + half)
        results = []
        for level in range(0, deep, ROWS):
            source = [forced[pair, level : level + ROWS, :] for pair in range(2)]
            moved = [
                base_ref[t, variable, level : level + ROWS, :]
                + pick(source[variable % 2], spots[variable])
                for variable in range(variables)
            ]
            excess = moved[1] - SATURATION_BASE * jnp.exp(SATURATION_SLOPE * moved[0])
            soft = jnp.maximum(excess, 0.0) + jnp.log(1.0 + jnp.exp(-jnp.abs(excess)))
            condensed = CONDENSE_RATE * soft
            updated = (
                moved[0] + condensed,
                moved[1] - condensed,
                RETAIN * moved[2] + condensed,
                moved[3],
            )
            count = min(ROWS, clev - level)
            for variable in range(variables):
                begin = level * plane + variables * t + variable
                flat_ref[pl.ds(begin, count, stride=plane), :] = updated[variable][:count]
            results.append(condensed)
        return results

    def store(begin, count):
        here = pl.ds(begin, count)
        return pltpu.make_async_copy(next_ref.at[:, here], next_hbm.at[:, here], sem)

    def advance(step, carry):
        results = [tile(WIDE * step + n) for n in range(WIDE)]
        store(WIDE * step, WIDE).start()
        sums[...] += pooled_sum(results, pool_ref[step])
        return carry

    lax.fori_loop(0, steps, advance, 0)
    lower = lane_ids(clev) < half
    extra = sums[0:clev]
    share = 1.0 / TIME_STEP
    first = mean_ref[0, 0:clev] + jnp.where(lower, share, share * RETAIN) * forced[0, 0:clev]
    first = first + extra
    second = mean_ref[1, 0:clev] + share * forced[1, 0:clev] - jnp.where(lower, extra, 0.0)
    feedback = lax.dot_general(
        up_ref[...],
        jnp.concatenate([first, second], axis=1),
        (((0,), (0,)), ((), ())),
        precision=EXACT,
    )
    for pair in range(2):
        for part in range(depth):
            for first in range(0, used, ROWS):
                begin = used * part + first
                out_ref[pl.ds(ROWS * first + depth * pair + part, ROWS, stride=ROWS), :] = (
                    feedback[begin : begin + ROWS, LANES * pair : LANES * pair + LANES]
                )
    store(0, columns).wait()


def update_kernel(got_ref, partial_ref, out_ref, field, sorted_ref, share):
    tiles = field.shape[0]
    unpack_pairs(got_ref, field)

    def collect(p):
        place = row_of(partial_ref[p, 1], ORDER_ROW).astype(jnp.int32)
        for part, values in enumerate(reorder(field, p // 2 * 2, place)):
            sorted_ref[p, part] = values

    each(tiles, collect)
    swap_groups(sorted_ref, field, share)

    def finish(q):
        pack_pair(
            out_ref,
            q,
            partial_ref[q, 0] + TIME_STEP * field[q, 0],
            partial_ref[q, 1] + TIME_STEP * field[q, 1],
        )

    each(tiles, finish)


def unpack_kernel(got_ref, state_ref, depth):
    elements, variables, nodes, levels = state_ref.shape
    used = levels // depth
    for pair in range(variables // 2):
        by_level = jnp.concatenate(
            [
                got_ref[pl.ds(ROWS * first + depth * pair + part, ROWS, stride=ROWS), :]
                for part in range(depth)
                for first in range(0, used, ROWS)
            ],
            axis=0,
        )
        fields = by_level.T.reshape(2, elements, nodes, levels)
        state_ref[:, pair] = fields[0]
        state_ref[:, variables // 2 + pair] = fields[1]


def kernel_call(body, name, results, scratch, *operands, hbm_in=(), hbm_out=(), cost=None):
    spec = {True: pl.BlockSpec(memory_space=pltpu.HBM), False: pl.BlockSpec(memory_space=pltpu.VMEM)}
    operands = [
        pltpu.with_memory_space_constraint(value, pltpu.HBM) if n in hbm_in else value
        for n, value in enumerate(operands)
    ]
    return pl.pallas_call(
        body,
        name=name,
        out_shape=results,
        in_specs=[spec[n in hbm_in] for n in range(len(operands))],
        out_specs=tuple(spec[n in hbm_out] for n in range(len(results))),
        scratch_shapes=scratch,
        cost_estimate=cost,
        compiler_params=pltpu.CompilerParams(vmem_limit_bytes=KERNEL_VMEM),
    )(*operands)


def exchange(slots):
    return lax.all_to_all(slots, AXES, split_axis=0, concat_axis=0, tiled=True)


def shards(
    model_state,
    cloud_state,
    neighbor,
    facing_edge,
    column_order,
    model_to_cloud_levels,
    cloud_to_model_levels,
):
    elements, variables, nodes, levels = model_state.shape
    clev, width = cloud_state.shape[1:]
    devices = lax.axis_size(AXES)
    block = column_order.shape[1]
    share = block // lax.axis_size("cols")
    depth = -(-levels // devices)
    assert variables == 4 and nodes == NODES and 2 * elements * nodes == LANES
    assert 2 * depth <= FAR_ROW and levels % (ROWS * depth) == 0 and block == 2 * LANES
    tiles = devices // 2
    f32 = jnp.float32
    shape = jax.ShapeDtypeStruct
    flat = shape((devices * ROWS, LANES), f32)
    slots = shape((devices, ROWS, LANES), f32)
    pairs = shape((tiles, 2, ROWS, LANES), f32)
    columns = width // LANES
    assert columns % WIDE == 0 and columns % 2 == 0
    deep = -(-clev // ROWS) * ROWS
    dma = pltpu.SemaphoreType.DMA

    packed, weights = kernel_call(
        functools.partial(pack_kernel, depth=depth, block=block),
        "pack_state",
        (flat, shape((2, LANES, 2 * LANES), jnp.bfloat16)),
        [
            pltpu.SMEM(neighbor.shape, jnp.int32),
            pltpu.SMEM(facing_edge.shape, jnp.int32),
            pltpu.VMEM(column_order.shape, jnp.int32),
            pltpu.VMEM(model_state.shape, f32),
            pltpu.VMEM((2, ROWS, block), f32),
            dma((5,)),
        ],
        neighbor,
        facing_edge,
        column_order,
        model_state,
        node_weights(),
        hbm_in=range(5),
    )
    by_level = exchange(packed.reshape(slots.shape))
    arranged, partial = kernel_call(
        functools.partial(tendency_kernel, depth=depth, share=share),
        "tendency",
        (slots, pairs),
        [
            pltpu.VMEM(pairs.shape, f32),
            pltpu.VMEM((tiles, 2, ROWS, 2 * LANES), f32),
            pltpu.VMEM(pairs.shape, f32),
            pltpu.VMEM(pairs.shape, f32),
        ],
        by_level,
        weights,
    )
    by_tile = cloud_state.reshape(variables, clev, columns, LANES).transpose(1, 2, 0, 3)
    base, mean, pool, down, up = kernel_call(
        settle_kernel,
        "settle",
        (
            shape((columns, variables, deep, LANES), f32),
            shape((2, deep, LANES), f32),
            shape((columns // WIDE, WIDE * LANES, LANES), jnp.bfloat16),
            shape((clev, levels), f32),
            shape((clev, levels), f32),
        ),
        [
            pltpu.VMEM((deep + 2, columns + 1, variables, LANES), f32),
            pltpu.VMEM((variables * deep, LANES), f32),
            dma((columns // WIDE + 2,)),
        ],
        by_tile,
        model_to_cloud_levels,
        cloud_to_model_levels.T,
        hbm_in=range(3),
        cost=pl.CostEstimate(flops=10**8, bytes_accessed=4 * 10**6, transcendentals=0),
    )
    by_column = exchange(arranged)
    cloud_next, fed = kernel_call(
        functools.partial(cloud_kernel, depth=depth),
        "cloud",
        (shape(by_tile.shape, f32), flat),
        [
            pltpu.VMEM((2, deep, LANES), f32),
            pltpu.VMEM((deep, LANES), f32),
            pltpu.VMEM((clev, columns + 1, variables, LANES), f32),
            dma,
        ],
        by_column.reshape(flat.shape),
        base,
        mean,
        pool,
        down,
        up,
        hbm_out=(0,),
    )
    fed_level = exchange(fed.reshape(slots.shape))
    (advanced,) = kernel_call(
        functools.partial(update_kernel, share=share),
        "update",
        (slots,),
        [pltpu.VMEM(pairs.shape, f32), pltpu.VMEM(pairs.shape, f32)],
        fed_level,
        partial,
    )
    home = exchange(advanced)
    (model_next,) = kernel_call(
        functools.partial(unpack_kernel, depth=depth),
        "unpack_state",
        (shape(model_state.shape, f32),),
        [],
        home.reshape(flat.shape),
    )
    cloud_next = cloud_next.transpose(2, 0, 1, 3).reshape(cloud_state.shape)
    return (model_next, cloud_next)


def solution(mesh):
    placed = (
        P(AXES, None, None, None),
        P(None, None, AXES),
        P(AXES, None),
        P(AXES, None),
        P("cols", None),
        P(),
        P(),
    )
    return jax.shard_map(
        shards,
        mesh=mesh,
        in_specs=placed,
        out_specs=(P(AXES, None, None, None), P(None, None, AXES)),
        check_vma=False,
    )
```

```python
import functools

import jax
import jax.numpy as jnp
import numpy as np
from jax import lax
from jax.experimental import pallas as pl
from jax.experimental.pallas import tpu as pltpu
from jax.sharding import PartitionSpec as P

CCOL = 32
NODES = 16
LANES = 128
ROWS = 8
AXES = ("cols", "vars")
VISCOSITY = 0.01
DRIFT = 0.05
PENALTY = 0.5
TIME_STEP = 0.5
CLOUD_ADVECT = 0.25
CLOUD_DIFFUSE = 0.1
CONDENSE_RATE = 0.3
SATURATION_BASE = 0.5
SATURATION_SLOPE = 0.3
RETAIN = 0.8
LOG2_E = 1.4426950408889634
EXACT = lax.Precision.HIGHEST
KERNEL_VMEM = 16 * 2**20
WIDE = 8
PIECE = 2
GROUP = 16
SWAPS = 4
FAR_ROW = 6
ORDER_ROW = 7


def lobatto_derivative():
    points = np.array([-1.0, -1.0 / np.sqrt(5.0), 1.0 / np.sqrt(5.0), 1.0])
    derivative = np.zeros((4, 4))
    for target in range(4):
        for source in range(4):
            if target != source:
                weight_target = np.prod(
                    [points[target] - points[middle] for middle in range(4) if middle != target]
                )
                weight_source = np.prod(
                    [points[source] - points[middle] for middle in range(4) if middle != source]
                )
                derivative[target, source] = weight_target / (
                    weight_source * (points[target] - points[source])
                )
        derivative[target, target] = np.sum(
            [1.0 / (points[target] - points[middle]) for middle in range(4) if middle != target]
        )
    return derivative


def node_weights():
    derivative = lobatto_derivative()
    along_first = np.kron(np.eye(4), derivative)
    along_second = np.kron(derivative, np.eye(4))
    laplace = along_first @ along_first + along_second @ along_second
    edges = np.zeros((4, 4))
    edges[0, :] += 1.0
    edges[3, :] += 1.0
    edges[:, 0] += 1.0
    edges[:, 3] += 1.0
    linear = VISCOSITY * laplace - PENALTY * np.diag(edges.reshape(-1))
    repeat = np.eye(LANES // NODES)
    weights = np.concatenate(
        [np.kron(repeat, linear.T), np.kron(repeat, -DRIFT * along_first.T)], axis=1
    )
    high = weights.astype(jnp.bfloat16)
    low = (weights - high.astype(np.float64)).astype(jnp.bfloat16)
    return jnp.asarray(np.stack([high, low]))


def each(count, body, group=GROUP):
    group = min(group, count)
    if count <= group:
        for index in range(count):
            body(index)
        return

    def several(first, carry):
        for n in range(group):
            body(first * group + n)
        return carry

    lax.fori_loop(0, count // group, several, 0)


def lane_ids(rows=ROWS):
    return lax.broadcasted_iota(jnp.int32, (rows, LANES), 1)


def row_ids():
    return lax.broadcasted_iota(jnp.int32, (ROWS, LANES), 0)


def pick(values, lanes):
    return jnp.take_along_axis(values, lanes, axis=1, mode="promise_in_bounds")


def half_turn(values):
    return pltpu.roll(values, LANES // 2, 1)


def slot_rows(slot, rows):
    return pl.ds(slot * rows, rows)


def split_pair(first, second):
    lower = lane_ids(first.shape[0]) < LANES // 2
    return (
        jnp.where(lower, first, half_turn(second)),
        jnp.where(lower, half_turn(first), second),
    )


def row_of(values, row):
    return jnp.broadcast_to(values[row : row + 1], (ROWS, LANES))


def unpack_pairs(got_ref, field):
    rows = got_ref.shape[0] // (2 * field.shape[0])

    def unpack(q):
        low, high = split_pair(
            got_ref[slot_rows(2 * q, rows), :], got_ref[slot_rows(2 * q + 1, rows), :]
        )
        field[q, 0, :rows] = low
        field[q, 1, :rows] = high

    each(field.shape[0], unpack)


def pack_pair(out_ref, q, rows, low, high):
    first, second = split_pair(low, high)
    out_ref[slot_rows(2 * q, rows), :] = first[:rows]
    out_ref[slot_rows(2 * q + 1, rows), :] = second[:rows]


def swap_groups(source, target, share):
    groups = LANES // share
    group = lane_ids() // share

    def swap(index):
        x = index // 2
        y = index % 2

        def gather(w):
            for part in range(2):
                joined = source[2 * groups * x + y, part]
                joined = pltpu.roll(joined, (LANES - share * w) % LANES, 1)
                for u in range(1, groups):
                    other = source[2 * (groups * x + u) + y, part]
                    turned = pltpu.roll(other, (share * (u + groups - w)) % LANES, 1)
                    joined = jnp.where(group == u, turned, joined)
                target[2 * (groups * y + w) + x, part] = joined

        each(groups, gather)

    each(4, swap, SWAPS)


def reorder(source, block_tile, places):
    spot = places & (LANES - 1)
    first = places < LANES
    return [
        jnp.where(
            first,
            pick(source[block_tile, part], spot),
            pick(source[block_tile + 1, part], spot),
        )
        for part in range(2)
    ]


def pack_kernel(
    nbr_hbm,
    face_hbm,
    order_hbm,
    state_hbm,
    weight_hbm,
    out_ref,
    weight_ref,
    nbr_ref,
    face_ref,
    order_ref,
    state_ref,
    scratch,
    sems,
    depth,
    block,
):
    copies = [
        pltpu.make_async_copy(source, target, sems.at[n])
        for n, (source, target) in enumerate(
            (
                (nbr_hbm, nbr_ref),
                (face_hbm, face_ref),
                (order_hbm, order_ref),
                (state_hbm, state_ref),
                (weight_hbm, weight_ref),
            )
        )
    ]
    for copy in copies:
        copy.start()
    elements, variables, nodes, levels = state_ref.shape
    used = levels // depth
    half = LANES // 2
    lane = lane_ids()
    own = lax.axis_index("vars")
    column = lane % half
    elem = column // nodes
    along_y = (column // 4) % 4
    along_x = column % 4
    upper = lane >= half
    edge = jnp.where(
        upper,
        jnp.where(along_x == 3, 1, jnp.where(along_x == 0, 3, -1)),
        jnp.where(along_y == 0, 0, jnp.where(along_y == 3, 2, -1)),
    )
    along = jnp.where(upper, along_y, along_x)
    place = jnp.where(edge >= 2, 3 - along, along)
    out_ref[...] = jnp.zeros_like(out_ref)
    copies[0].wait()
    copies[1].wait()
    far = jnp.zeros_like(lane)
    face = jnp.zeros_like(lane)
    for e in range(elements):
        for j in range(4):
            here = (elem == e) & (edge == j)
            far = jnp.where(here, nbr_ref[e, j], far)
            face = jnp.where(here, face_ref[e, j], face)
    node = jnp.where(
        face == 0,
        3 - place,
        jnp.where(face == 1, 15 - 4 * place, jnp.where(face == 2, 12 + place, 4 * place)),
    )
    far_col = jnp.where(edge >= 0, nodes * far + node, -1).astype(jnp.float32)

    copies[2].wait()
    order = order_ref[...]
    spots = lax.broadcasted_iota(jnp.int32, (block, block), 0)
    marks = (spots == order).astype(jnp.float32).astype(jnp.bfloat16)
    numbers = lax.broadcasted_iota(jnp.int32, (ROWS, block), 1).astype(jnp.float32)
    scratch[0] = jnp.broadcast_to(order, (ROWS, block)).astype(jnp.float32)
    scratch[1] = lax.dot_general(
        numbers.astype(jnp.bfloat16),
        marks,
        (((1,), (1,)), ((), ())),
        preferred_element_type=jnp.float32,
    )
    begin = pl.multiple_of((own // 2) * LANES, LANES)
    order_part = scratch[0, :, pl.ds(begin, LANES)]
    place_part = scratch[1, :, pl.ds(begin, LANES)]
    odd = own % 2 == 1
    order_part = jnp.where(odd, half_turn(order_part), order_part)
    place_part = jnp.where(odd, place_part, half_turn(place_part))
    indices = jnp.where(upper, place_part, order_part)

    slots = out_ref.shape[0] // ROWS
    for first in range(0, slots, ROWS):
        out_ref[pl.ds(ROWS * first + FAR_ROW, ROWS, stride=ROWS), :] = far_col
        out_ref[pl.ds(ROWS * first + ORDER_ROW, ROWS, stride=ROWS), :] = indices
    copies[3].wait()
    for pair in range(variables // 2):
        fields = jnp.concatenate(
            [
                state_ref[:, pair].reshape(elements * nodes, levels),
                state_ref[:, variables // 2 + pair].reshape(elements * nodes, levels),
            ],
            axis=0,
        )
        by_level = fields.T
        for part in range(depth):
            for first in range(0, used, ROWS):
                begin = used * part + first
                out_ref[pl.ds(ROWS * first + depth * pair + part, ROWS, stride=ROWS), :] = (
                    by_level[begin : begin + ROWS]
                )
    copies[4].wait()


def tendency_kernel(
    got_ref, weight_ref, out_ref, partial_ref, field, linear, tend, moved, depth, share
):
    tiles = field.shape[0]
    row = row_ids()
    lower = lane_ids() < LANES // 2
    unpack_pairs(got_ref, field)
    step = min(tiles, 16)

    def multiply(chunk):
        fields = field[pl.ds(chunk * step, step)].reshape(step * 2 * ROWS, LANES)
        high, low = in_two(fields)
        coarse, fine = weight_ref[0], weight_ref[1]
        result = jnp.dot(
            jnp.concatenate([high, low], axis=1),
            jnp.concatenate([coarse, coarse], axis=0),
            preferred_element_type=jnp.float32,
        ) + jnp.dot(high, fine, preferred_element_type=jnp.float32)
        linear[pl.ds(chunk * step, step)] = result.reshape(step, 2, ROWS, 2 * LANES)

    each(tiles // step, multiply, 1)

    def advance(q):
        before = jnp.where(q == 0, tiles - 1, q - 1)
        after = jnp.where(q == tiles - 1, 0, q + 1)
        high = field[q, 1]
        wind = jnp.where(row < depth, pltpu.roll(high, ROWS - depth, 0), high)
        sums = [0.0, 0.0]
        for side in range(2):
            far = row_of(field[q, side], FAR_ROW).astype(jnp.int32)
            spot = far & (LANES - 1)
            inside = lax.shift_right_arithmetic(far, 7) == q
            for part in range(2):
                beside = jnp.where(lower, field[after, part], field[before, part])
                value = jnp.where(inside, pick(field[q, part], spot), pick(beside, spot))
                sums[part] = sums[part] + jnp.where(far >= 0, value, 0.0)
        for part in range(2):
            own = field[q, part]
            result = (
                linear[q, part, :, :LANES]
                + wind * linear[q, part, :, LANES:]
                + PENALTY * sums[part]
            )
            tend[q, part] = result
            partial_ref[q, part] = jnp.where(row < FAR_ROW, own + TIME_STEP * result, own)

    each(tiles, advance)
    swap_groups(tend, moved, share)

    def arrange(p):
        order = row_of(field[p, 0], ORDER_ROW).astype(jnp.int32)
        pack_pair(out_ref, p, 2 * depth, *reorder(moved, p // 2 * 2, order))

    each(tiles, arrange)


def in_two(values):
    high = values.astype(jnp.bfloat16)
    low = (values - high.astype(jnp.float32)).astype(jnp.bfloat16)
    return high, low


def pool_weights(step):
    wide = WIDE * LANES
    lane = lax.broadcasted_iota(jnp.int32, (wide, LANES), 1) % (LANES // 2)
    owner = lax.broadcasted_iota(jnp.int32, (wide, LANES), 0) // CCOL
    mean = 1.0 / (CCOL * TIME_STEP)
    return jnp.where(lane == (wide // CCOL) * step + owner, mean, 0.0).astype(jnp.bfloat16)


def pooled_sum(tiles, weights):
    joined = jnp.concatenate([jnp.concatenate(tile, axis=0) for tile in tiles], axis=1)
    rows = joined.shape[0]
    both = jnp.concatenate(in_two(joined), axis=0)
    result = jnp.dot(both, weights, preferred_element_type=jnp.float32)
    return result[:rows] + result[rows:]


def settle_kernel(
    cloud_hbm,
    down_hbm,
    up_hbm,
    base_ref,
    mean_ref,
    pool_ref,
    spread_ref,
    down_ref,
    up_ref,
    cloud_ref,
    sums,
    sems,
):
    columns, variables, deep = base_ref.shape[:3]
    clev = cloud_hbm.shape[0]
    plane = (columns + 1) * variables
    steps = columns // WIDE
    small = [
        pltpu.make_async_copy(down_hbm, down_ref, sems.at[columns // PIECE]),
        pltpu.make_async_copy(up_hbm, up_ref, sems.at[columns // PIECE + 1]),
    ]

    def fetch(step):
        here = pl.ds(PIECE * step, PIECE)
        return pltpu.make_async_copy(
            cloud_hbm.at[:, here], cloud_ref.at[pl.ds(1, clev), here], sems.at[step]
        )

    pieces = columns // PIECE
    for step in range(pieces):
        fetch(step).start()
    for copy in small:
        copy.start()
    flat_ref = cloud_ref.reshape((deep + 2) * plane, LANES)
    rim = jnp.zeros((plane, LANES), jnp.float32)
    flat_ref[0:plane] = rim
    for level in range(clev, deep + 1):
        flat_ref[(level + 1) * plane : (level + 2) * plane] = rim
    sums[...] = jnp.zeros_like(sums)
    column = lax.broadcasted_iota(jnp.int32, spread_ref.shape, 0) % LANES
    place = lax.broadcasted_iota(jnp.int32, spread_ref.shape, 1)
    column_of = (LANES // 2) * (place // LANES) + place % LANES // CCOL
    spread_ref[...] = jnp.where(column == column_of, 1.0, 0.0).astype(jnp.bfloat16)
    lane = lane_ids()
    start = lane // CCOL * CCOL
    next_lane = start + (lane + 1) % CCOL
    last_lane = start + (lane + CCOL - 1) % CCOL

    def tile(t):
        def load(level, variable):
            begin = (level + 1) * plane + variables * t + variable
            return flat_ref[pl.ds(begin, ROWS, stride=plane), :]

        changes = []
        winds = [
            (-CLOUD_ADVECT * TIME_STEP) * load(level, 3) for level in range(0, deep, ROWS)
        ]
        for variable in range(variables):
            for level in range(0, deep, ROWS):
                now = load(level, variable)
                ahead = pick(now, next_lane)
                behind = pick(now, last_lane)
                around = load(level - 1, variable) + load(level + 1, variable)
                change = winds[level // ROWS] * (ahead - behind) + (
                    CLOUD_DIFFUSE * TIME_STEP
                ) * (around - 2.0 * now)
                base = now + change
                base_ref[t, variable, level : level + ROWS, :] = base
                changes.append(RETAIN * base - now if variable == 2 else change)
        return changes

    def advance(step, carry):
        weights = pool_weights(step)
        pool_ref[step] = weights
        results = []
        for n in range(WIDE):
            if n % PIECE == 0:
                fetch((WIDE // PIECE) * step + n // PIECE).wait()
            results.append(tile(WIDE * step + n))
        sums[...] += pooled_sum(results, weights)
        return carry

    lax.fori_loop(0, steps, advance, 0)
    lower = lane_ids(deep) < LANES // 2
    for pair in range(2):
        mean_ref[pair] = jnp.where(
            lower,
            sums[deep * pair : deep * (pair + 1)],
            sums[deep * (2 + pair) : deep * (3 + pair)],
        )
    for copy in small:
        copy.wait()


def cloud_kernel(
    got_ref,
    base_ref,
    mean_ref,
    pool_ref,
    spread_ref,
    down_ref,
    up_ref,
    next_hbm,
    out_ref,
    forced,
    sums,
    next_ref,
    sem,
    depth,
):
    columns, variables, deep = base_ref.shape[:3]
    clev, levels = down_ref.shape
    plane = (columns + 1) * variables
    flat_ref = next_ref.reshape(clev * plane, LANES)
    steps = columns // WIDE
    used = levels // depth
    rows = 2 * depth
    half = LANES // 2
    fields = jnp.concatenate(
        [
            jnp.concatenate(
                [
                    got_ref[pl.ds(rows * first + depth * pair + part, ROWS, stride=rows), :]
                    for part in range(depth)
                    for first in range(0, used, ROWS)
                ],
                axis=0,
            )
            for pair in range(2)
        ],
        axis=1,
    )
    forcing = jnp.dot(TIME_STEP * down_ref[...], fields, precision=EXACT)
    for pair in range(2):
        forced[pair, 0:clev] = forcing[:, LANES * pair : LANES * pair + LANES]
        forced[pair, clev:deep] = jnp.zeros((deep - clev, LANES), jnp.float32)
    sums[...] = jnp.zeros_like(sums)
    high, low = in_two(jnp.concatenate([forced[0], forced[1]], axis=0))

    def tile(t):
        shift = LANES - (LANES // CCOL) * t
        turned = [pltpu.roll(values, shift, 1) for values in (high, low)]
        push = jnp.dot(
            jnp.concatenate(turned, axis=1).astype(jnp.bfloat16),
            spread_ref[...],
            preferred_element_type=jnp.float32,
        )
        results = []
        for level in range(0, deep, ROWS):
            moved = []
            for variable in range(variables):
                begin = deep * (variable % 2) + level
                lanes = LANES * (variable // 2)
                moved.append(
                    base_ref[t, variable, level : level + ROWS, :]
                    + push[begin : begin + ROWS, lanes : lanes + LANES]
                )
            excess = moved[1] - SATURATION_BASE * jnp.exp2((SATURATION_SLOPE * LOG2_E) * moved[0])
            soft = jnp.maximum(excess, 0.0) + jnp.log(1.0 + jnp.exp2(-LOG2_E * jnp.abs(excess)))
            condensed = CONDENSE_RATE * soft
            updated = (
                moved[0] + condensed,
                moved[1] - condensed,
                RETAIN * moved[2] + condensed,
                moved[3],
            )
            count = min(ROWS, clev - level)
            for variable in range(variables):
                begin = level * plane + variables * t + variable
                flat_ref[pl.ds(begin, count, stride=plane), :] = updated[variable][:count]
            results.append(condensed)
        return results

    def store(begin, count):
        here = pl.ds(begin, count)
        return pltpu.make_async_copy(next_ref.at[:, here], next_hbm.at[:, here], sem)

    def advance(step, carry):
        results = []
        for n in range(WIDE):
            results.append(tile(WIDE * step + n))
            if (n + 1) % PIECE == 0:
                store(WIDE * step + n + 1 - PIECE, PIECE).start()
        sums[...] += pooled_sum(results, pool_ref[step])
        return carry

    lax.fori_loop(0, steps, advance, 0)
    lower = lane_ids(clev) < half
    extra = sums[0:clev]
    share = 1.0 / TIME_STEP
    first = mean_ref[0, 0:clev] + jnp.where(lower, share, share * RETAIN) * forced[0, 0:clev]
    first = first + extra
    second = mean_ref[1, 0:clev] + share * forced[1, 0:clev] - jnp.where(lower, extra, 0.0)
    feedback = lax.dot_general(
        up_ref[...],
        jnp.concatenate([first, second], axis=1),
        (((0,), (0,)), ((), ())),
        precision=EXACT,
    )
    for pair in range(2):
        for part in range(depth):
            for first in range(0, used, ROWS):
                begin = used * part + first
                out_ref[pl.ds(rows * first + depth * pair + part, ROWS, stride=rows), :] = (
                    feedback[begin : begin + ROWS, LANES * pair : LANES * pair + LANES]
                )
    store(0, columns).wait()


def update_kernel(got_ref, partial_ref, out_ref, field, sorted_ref, share):
    tiles = field.shape[0]
    rows = got_ref.shape[0] // (2 * tiles)
    unpack_pairs(got_ref, field)

    def collect(p):
        place = row_of(partial_ref[p, 1], ORDER_ROW).astype(jnp.int32)
        for part, values in enumerate(reorder(field, p // 2 * 2, place)):
            sorted_ref[p, part] = values

    each(tiles, collect)
    swap_groups(sorted_ref, field, share)

    def finish(q):
        pack_pair(
            out_ref,
            q,
            rows,
            partial_ref[q, 0] + TIME_STEP * field[q, 0],
            partial_ref[q, 1] + TIME_STEP * field[q, 1],
        )

    each(tiles, finish)


def unpack_kernel(got_ref, state_ref, depth):
    elements, variables, nodes, levels = state_ref.shape
    used = levels // depth
    for pair in range(variables // 2):
        by_level = jnp.concatenate(
            [
                got_ref[pl.ds(2 * depth * first + depth * pair + part, ROWS, stride=2 * depth), :]
                for part in range(depth)
                for first in range(0, used, ROWS)
            ],
            axis=0,
        )
        fields = by_level.T.reshape(2, elements, nodes, levels)
        state_ref[:, pair] = fields[0]
        state_ref[:, variables // 2 + pair] = fields[1]


def kernel_call(body, name, results, scratch, *operands, hbm_in=(), hbm_out=(), cost=None):
    spec = {True: pl.BlockSpec(memory_space=pltpu.HBM), False: pl.BlockSpec(memory_space=pltpu.VMEM)}
    operands = [
        pltpu.with_memory_space_constraint(value, pltpu.HBM) if n in hbm_in else value
        for n, value in enumerate(operands)
    ]
    return pl.pallas_call(
        body,
        name=name,
        out_shape=results,
        in_specs=[spec[n in hbm_in] for n in range(len(operands))],
        out_specs=tuple(spec[n in hbm_out] for n in range(len(results))),
        scratch_shapes=scratch,
        cost_estimate=cost,
        compiler_params=pltpu.CompilerParams(vmem_limit_bytes=KERNEL_VMEM),
    )(*operands)


def exchange(values, devices):
    slots = values.reshape(devices, values.shape[0] // devices, 1, LANES)
    moved = lax.all_to_all(slots, AXES, split_axis=0, concat_axis=0, tiled=True)
    return moved.reshape(values.shape)


def shards(
    model_state,
    cloud_state,
    neighbor,
    facing_edge,
    column_order,
    model_to_cloud_levels,
    cloud_to_model_levels,
):
    elements, variables, nodes, levels = model_state.shape
    clev, width = cloud_state.shape[1:]
    devices = lax.axis_size(AXES)
    block = column_order.shape[1]
    share = block // lax.axis_size("cols")
    depth = -(-levels // devices)
    assert variables == 4 and nodes == NODES and 2 * elements * nodes == LANES
    assert 2 * depth <= FAR_ROW and levels % (ROWS * depth) == 0 and block == 2 * LANES
    tiles = devices // 2
    f32 = jnp.float32
    shape = jax.ShapeDtypeStruct
    flat = shape((devices * ROWS, LANES), f32)
    rows = shape((devices * 2 * depth, LANES), f32)
    pairs = shape((tiles, 2, ROWS, LANES), f32)
    columns = width // LANES
    assert columns % WIDE == 0 and WIDE % PIECE == 0
    deep = -(-clev // ROWS) * ROWS
    dma = pltpu.SemaphoreType.DMA

    packed, weights = kernel_call(
        functools.partial(pack_kernel, depth=depth, block=block),
        "pack_state",
        (flat, shape((2, LANES, 2 * LANES), jnp.bfloat16)),
        [
            pltpu.SMEM(neighbor.shape, jnp.int32),
            pltpu.SMEM(facing_edge.shape, jnp.int32),
            pltpu.VMEM(column_order.shape, jnp.int32),
            pltpu.VMEM(model_state.shape, f32),
            pltpu.VMEM((2, ROWS, block), f32),
            dma((5,)),
        ],
        neighbor,
        facing_edge,
        column_order,
        model_state,
        node_weights(),
        hbm_in=range(5),
    )
    by_level = exchange(packed, devices)
    arranged, partial = kernel_call(
        functools.partial(tendency_kernel, depth=depth, share=share),
        "tendency",
        (rows, pairs),
        [
            pltpu.VMEM(pairs.shape, f32),
            pltpu.VMEM((tiles, 2, ROWS, 2 * LANES), f32),
            pltpu.VMEM(pairs.shape, f32),
            pltpu.VMEM(pairs.shape, f32),
        ],
        by_level,
        weights,
    )
    by_tile = cloud_state.reshape(variables, clev, columns, LANES).transpose(1, 2, 0, 3)
    base, mean, pool, spread, down, up = kernel_call(
        settle_kernel,
        "settle",
        (
            shape((columns, variables, deep, LANES), f32),
            shape((2, deep, LANES), f32),
            shape((columns // WIDE, WIDE * LANES, LANES), jnp.bfloat16),
            shape((2 * LANES, 2 * LANES), jnp.bfloat16),
            shape((clev, levels), f32),
            shape((clev, levels), f32),
        ),
        [
            pltpu.VMEM((deep + 2, columns + 1, variables, LANES), f32),
            pltpu.VMEM((variables * deep, LANES), f32),
            dma((columns // PIECE + 2,)),
        ],
        by_tile,
        model_to_cloud_levels,
        cloud_to_model_levels.T,
        hbm_in=range(3),
        cost=pl.CostEstimate(flops=10**8, bytes_accessed=4 * 10**6, transcendentals=0),
    )
    by_column = exchange(arranged, devices)
    cloud_next, fed = kernel_call(
        functools.partial(cloud_kernel, depth=depth),
        "cloud",
        (shape(by_tile.shape, f32), rows),
        [
            pltpu.VMEM((2, deep, LANES), f32),
            pltpu.VMEM((deep, LANES), f32),
            pltpu.VMEM((clev, columns + 1, variables, LANES), f32),
            dma,
        ],
        by_column,
        base,
        mean,
        pool,
        spread,
        down,
        up,
        hbm_out=(0,),
    )
    fed_level = exchange(fed, devices)
    (advanced,) = kernel_call(
        functools.partial(update_kernel, share=share),
        "update",
        (rows,),
        [pltpu.VMEM(pairs.shape, f32), pltpu.VMEM(pairs.shape, f32)],
        fed_level,
        partial,
    )
    home = exchange(advanced, devices)
    (model_next,) = kernel_call(
        functools.partial(unpack_kernel, depth=depth),
        "unpack_state",
        (shape(model_state.shape, f32),),
        [],
        home,
    )
    cloud_next = cloud_next.transpose(2, 0, 1, 3).reshape(cloud_state.shape)
    return (model_next, cloud_next)


def solution(mesh):
    placed = (
        P(AXES, None, None, None),
        P(None, None, AXES),
        P(AXES, None),
        P(AXES, None),
        P("cols", None),
        P(),
        P(),
    )
    return jax.shard_map(
        shards,
        mesh=mesh,
        in_specs=placed,
        out_specs=(P(AXES, None, None, None), P(None, None, AXES)),
        check_vma=False,
    )
```

```python
import functools

import jax
import jax.numpy as jnp
import numpy as np
from jax import lax
from jax.experimental import pallas as pl
from jax.experimental.pallas import tpu as pltpu
from jax.sharding import PartitionSpec as P

CCOL = 32
NODES = 16
LANES = 128
ROWS = 8
AXES = ("cols", "vars")
VISCOSITY = 0.01
DRIFT = 0.05
PENALTY = 0.5
TIME_STEP = 0.5
CLOUD_ADVECT = 0.25
CLOUD_DIFFUSE = 0.1
CONDENSE_RATE = 0.3
SATURATION_BASE = 0.5
SATURATION_SLOPE = 0.3
RETAIN = 0.8
LOG2_E = 1.4426950408889634
EXACT = lax.Precision.HIGHEST
KERNEL_VMEM = 16 * 2**20
WIDE = 8
PIECE = 2
GROUP = 16
SWAPS = 4


def lobatto_derivative():
    points = np.array([-1.0, -1.0 / np.sqrt(5.0), 1.0 / np.sqrt(5.0), 1.0])
    derivative = np.zeros((4, 4))
    for target in range(4):
        for source in range(4):
            if target != source:
                weight_target = np.prod(
                    [points[target] - points[middle] for middle in range(4) if middle != target]
                )
                weight_source = np.prod(
                    [points[source] - points[middle] for middle in range(4) if middle != source]
                )
                derivative[target, source] = weight_target / (
                    weight_source * (points[target] - points[source])
                )
        derivative[target, target] = np.sum(
            [1.0 / (points[target] - points[middle]) for middle in range(4) if middle != target]
        )
    return derivative


def node_weights():
    derivative = lobatto_derivative()
    along_first = np.kron(np.eye(4), derivative)
    along_second = np.kron(derivative, np.eye(4))
    laplace = along_first @ along_first + along_second @ along_second
    edges = np.zeros((4, 4))
    edges[0, :] += 1.0
    edges[3, :] += 1.0
    edges[:, 0] += 1.0
    edges[:, 3] += 1.0
    linear = VISCOSITY * laplace - PENALTY * np.diag(edges.reshape(-1))
    repeat = np.eye(LANES // NODES)
    weights = np.concatenate(
        [np.kron(repeat, linear.T), np.kron(repeat, -DRIFT * along_first.T)], axis=1
    )
    high = weights.astype(jnp.bfloat16)
    low = (weights - high.astype(np.float64)).astype(jnp.bfloat16)
    return jnp.asarray(np.stack([high, low]))


def each(count, body, group=GROUP):
    group = min(group, count)
    if count <= group:
        for index in range(count):
            body(index)
        return

    def several(first, carry):
        for n in range(group):
            body(first * group + n)
        return carry

    lax.fori_loop(0, count // group, several, 0)


def lane_ids(rows=ROWS):
    return lax.broadcasted_iota(jnp.int32, (rows, LANES), 1)


def row_ids():
    return lax.broadcasted_iota(jnp.int32, (ROWS, LANES), 0)


def pick(values, lanes):
    return jnp.take_along_axis(values, lanes, axis=1, mode="promise_in_bounds")


def half_turn(values):
    return pltpu.roll(values, LANES // 2, 1)


def slot_rows(slot, rows):
    return pl.ds(slot * rows, rows)


def split_pair(first, second):
    lower = lane_ids(first.shape[0]) < LANES // 2
    return (
        jnp.where(lower, first, half_turn(second)),
        jnp.where(lower, half_turn(first), second),
    )


def row_of(values, row):
    return jnp.broadcast_to(values[row : row + 1], (ROWS, LANES))


def far_row(whole):
    return 2 * whole + 1


def order_row(whole):
    return 2 * whole + 2


def scatter_levels(out_ref, pitch, whole, parts, with_wind=False):
    devices = out_ref.shape[0] // pitch
    levels = parts[0].shape[0]
    for pair in range(2):
        for turn in range(whole):
            for first in range(0, devices, ROWS):
                begin = turn * devices + first
                out_ref[pl.ds(pitch * first + 2 * turn + pair, ROWS, stride=pitch), :] = parts[
                    pair
                ][begin : begin + ROWS]
    for first in range(whole * devices, levels, ROWS):
        wind = parts[1][first : first + ROWS]
        for variable in range(4):
            values = parts[variable % 2][first : first + ROWS]
            if variable >= 2:
                values = half_turn(values)
            if with_wind:
                values = jnp.where(lane_ids() < LANES // 2, values, wind)
            begin = pitch * (4 * (first - whole * devices) + variable) + 2 * whole
            out_ref[pl.ds(begin, ROWS, stride=4 * pitch), :] = values


def gather_levels(got_ref, whole, levels):
    pitch = 2 * whole + 1
    devices = got_ref.shape[0] // pitch
    parts = []
    for pair in range(2):
        pieces = [
            got_ref[pl.ds(pitch * first + 2 * turn + pair, ROWS, stride=pitch), :]
            for turn in range(whole)
            for first in range(0, devices, ROWS)
        ]
        for first in range(whole * devices, levels, ROWS):
            lower, upper = (
                got_ref[
                    pl.ds(
                        pitch * (4 * (first - whole * devices) + variable) + 2 * whole,
                        ROWS,
                        stride=4 * pitch,
                    ),
                    :,
                ]
                for variable in (pair, 2 + pair)
            )
            pieces.append(jnp.where(lane_ids() < LANES // 2, lower, half_turn(upper)))
        parts.append(jnp.concatenate(pieces, axis=0))
    return parts


def unpack_pairs(got_ref, field):
    rows = got_ref.shape[0] // (2 * field.shape[0])

    def unpack(q):
        low, high = split_pair(
            got_ref[slot_rows(2 * q, rows), :], got_ref[slot_rows(2 * q + 1, rows), :]
        )
        field[q, 0, :rows] = low
        field[q, 1, :rows] = high

    each(field.shape[0], unpack)


def pack_pair(out_ref, q, rows, low, high):
    first, second = split_pair(low, high)
    out_ref[slot_rows(2 * q, rows), :] = first[:rows]
    out_ref[slot_rows(2 * q + 1, rows), :] = second[:rows]


def swap_groups(source, target, share):
    groups = LANES // share
    group = lane_ids() // share

    def swap(index):
        x = index // 2
        y = index % 2

        def gather(w):
            for part in range(2):
                joined = source[2 * groups * x + y, part]
                joined = pltpu.roll(joined, (LANES - share * w) % LANES, 1)
                for u in range(1, groups):
                    other = source[2 * (groups * x + u) + y, part]
                    turned = pltpu.roll(other, (share * (u + groups - w)) % LANES, 1)
                    joined = jnp.where(group == u, turned, joined)
                target[2 * (groups * y + w) + x, part] = joined

        each(groups, gather)

    each(4, swap, SWAPS)


def reorder(source, block_tile, places):
    spot = places & (LANES - 1)
    first = places < LANES
    return [
        jnp.where(
            first,
            pick(source[block_tile, part], spot),
            pick(source[block_tile + 1, part], spot),
        )
        for part in range(2)
    ]


def pack_kernel(
    nbr_hbm,
    face_hbm,
    order_hbm,
    state_hbm,
    weight_hbm,
    out_ref,
    weight_ref,
    nbr_ref,
    face_ref,
    order_ref,
    state_ref,
    scratch,
    sems,
    whole,
    block,
):
    copies = [
        pltpu.make_async_copy(source, target, sems.at[n])
        for n, (source, target) in enumerate(
            (
                (nbr_hbm, nbr_ref),
                (face_hbm, face_ref),
                (order_hbm, order_ref),
                (state_hbm, state_ref),
                (weight_hbm, weight_ref),
            )
        )
    ]
    for copy in copies:
        copy.start()
    elements, variables, nodes, levels = state_ref.shape
    half = LANES // 2
    lane = lane_ids()
    own = lax.axis_index("vars")
    column = lane % half
    elem = column // nodes
    along_y = (column // 4) % 4
    along_x = column % 4
    upper = lane >= half
    edge = jnp.where(
        upper,
        jnp.where(along_x == 3, 1, jnp.where(along_x == 0, 3, -1)),
        jnp.where(along_y == 0, 0, jnp.where(along_y == 3, 2, -1)),
    )
    along = jnp.where(upper, along_y, along_x)
    place = jnp.where(edge >= 2, 3 - along, along)
    out_ref[...] = jnp.zeros_like(out_ref)
    copies[0].wait()
    copies[1].wait()
    far = jnp.zeros_like(lane)
    face = jnp.zeros_like(lane)
    for e in range(elements):
        for j in range(4):
            here = (elem == e) & (edge == j)
            far = jnp.where(here, nbr_ref[e, j], far)
            face = jnp.where(here, face_ref[e, j], face)
    node = jnp.where(
        face == 0,
        3 - place,
        jnp.where(face == 1, 15 - 4 * place, jnp.where(face == 2, 12 + place, 4 * place)),
    )
    far_col = jnp.where(edge >= 0, nodes * far + node, -1).astype(jnp.float32)

    copies[2].wait()
    order = order_ref[...]
    spots = lax.broadcasted_iota(jnp.int32, (block, block), 0)
    marks = (spots == order).astype(jnp.float32).astype(jnp.bfloat16)
    numbers = lax.broadcasted_iota(jnp.int32, (ROWS, block), 1).astype(jnp.float32)
    scratch[0] = jnp.broadcast_to(order, (ROWS, block)).astype(jnp.float32)
    scratch[1] = lax.dot_general(
        numbers.astype(jnp.bfloat16),
        marks,
        (((1,), (1,)), ((), ())),
        preferred_element_type=jnp.float32,
    )
    begin = pl.multiple_of((own // 2) * LANES, LANES)
    order_part = scratch[0, :, pl.ds(begin, LANES)]
    place_part = scratch[1, :, pl.ds(begin, LANES)]
    odd = own % 2 == 1
    order_part = jnp.where(odd, half_turn(order_part), order_part)
    place_part = jnp.where(odd, place_part, half_turn(place_part))
    indices = jnp.where(upper, place_part, order_part)

    pitch = order_row(whole) + 1
    slots = out_ref.shape[0] // pitch
    for first in range(0, slots, ROWS):
        out_ref[pl.ds(pitch * first + far_row(whole), ROWS, stride=pitch), :] = far_col
        out_ref[pl.ds(pitch * first + order_row(whole), ROWS, stride=pitch), :] = indices
    copies[3].wait()
    parts = []
    for pair in range(variables // 2):
        fields = jnp.concatenate(
            [
                state_ref[:, pair].reshape(elements * nodes, levels),
                state_ref[:, variables // 2 + pair].reshape(elements * nodes, levels),
            ],
            axis=0,
        )
        parts.append(fields.T)
    scatter_levels(out_ref, pitch, whole, parts, with_wind=True)
    copies[4].wait()


def tendency_kernel(
    got_ref, weight_ref, out_ref, partial_ref, field, linear, tend, moved, whole, share
):
    tiles = field.shape[0]
    row = row_ids()
    lower = lane_ids() < LANES // 2
    wind_row = jnp.where(row < 2 * whole, row | 1, 2 * whole)
    unpack_pairs(got_ref, field)
    step = min(tiles, 16)

    def multiply(chunk):
        fields = field[pl.ds(chunk * step, step)].reshape(step * 2 * ROWS, LANES)
        high, low = in_two(fields)
        coarse, fine = weight_ref[0], weight_ref[1]
        result = jnp.dot(
            jnp.concatenate([high, low], axis=1),
            jnp.concatenate([coarse, coarse], axis=0),
            preferred_element_type=jnp.float32,
        ) + jnp.dot(high, fine, preferred_element_type=jnp.float32)
        linear[pl.ds(chunk * step, step)] = result.reshape(step, 2, ROWS, 2 * LANES)

    each(tiles // step, multiply, 1)

    def advance(q):
        before = jnp.where(q == 0, tiles - 1, q - 1)
        after = jnp.where(q == tiles - 1, 0, q + 1)
        high = field[q, 1]
        wind = jnp.take_along_axis(high, wind_row, axis=0, mode="promise_in_bounds")
        sums = [0.0, 0.0]
        for side in range(2):
            far = row_of(field[q, side], far_row(whole)).astype(jnp.int32)
            spot = far & (LANES - 1)
            inside = lax.shift_right_arithmetic(far, 7) == q
            for part in range(2):
                beside = jnp.where(lower, field[after, part], field[before, part])
                value = jnp.where(inside, pick(field[q, part], spot), pick(beside, spot))
                sums[part] = sums[part] + jnp.where(far >= 0, value, 0.0)
        for part in range(2):
            own = field[q, part]
            result = (
                linear[q, part, :, :LANES]
                + wind * linear[q, part, :, LANES:]
                + PENALTY * sums[part]
            )
            tend[q, part] = result
            partial_ref[q, part] = jnp.where(
                row < far_row(whole), own + TIME_STEP * result, own
            )

    each(tiles, advance)
    swap_groups(tend, moved, share)

    def arrange(p):
        order = row_of(field[p, 0], order_row(whole)).astype(jnp.int32)
        pack_pair(out_ref, p, far_row(whole), *reorder(moved, p // 2 * 2, order))

    each(tiles, arrange)


def in_two(values):
    high = values.astype(jnp.bfloat16)
    low = (values - high.astype(jnp.float32)).astype(jnp.bfloat16)
    return high, low


def pool_weights(step):
    wide = WIDE * LANES
    lane = lax.broadcasted_iota(jnp.int32, (wide, LANES), 1) % (LANES // 2)
    owner = lax.broadcasted_iota(jnp.int32, (wide, LANES), 0) // CCOL
    mean = 1.0 / (CCOL * TIME_STEP)
    return jnp.where(lane == (wide // CCOL) * step + owner, mean, 0.0).astype(jnp.bfloat16)


def pooled_sum(tiles, weights):
    joined = jnp.concatenate([jnp.concatenate(tile, axis=0) for tile in tiles], axis=1)
    rows = joined.shape[0]
    both = jnp.concatenate(in_two(joined), axis=0)
    result = jnp.dot(both, weights, preferred_element_type=jnp.float32)
    return result[:rows] + result[rows:]


def settle_kernel(
    cloud_hbm,
    down_hbm,
    up_hbm,
    base_ref,
    mean_ref,
    pool_ref,
    spread_ref,
    down_ref,
    up_ref,
    cloud_ref,
    sums,
    sems,
):
    columns, variables, deep = base_ref.shape[:3]
    clev = cloud_hbm.shape[0]
    plane = (columns + 1) * variables
    steps = columns // WIDE
    small = [
        pltpu.make_async_copy(down_hbm, down_ref, sems.at[columns // PIECE]),
        pltpu.make_async_copy(up_hbm, up_ref, sems.at[columns // PIECE + 1]),
    ]

    def fetch(step):
        here = pl.ds(PIECE * step, PIECE)
        return pltpu.make_async_copy(
            cloud_hbm.at[:, here], cloud_ref.at[pl.ds(1, clev), here], sems.at[step]
        )

    pieces = columns // PIECE
    for step in range(pieces):
        fetch(step).start()
    for copy in small:
        copy.start()
    flat_ref = cloud_ref.reshape((deep + 2) * plane, LANES)
    rim = jnp.zeros((plane, LANES), jnp.float32)
    flat_ref[0:plane] = rim
    for level in range(clev, deep + 1):
        flat_ref[(level + 1) * plane : (level + 2) * plane] = rim
    sums[...] = jnp.zeros_like(sums)
    column = lax.broadcasted_iota(jnp.int32, spread_ref.shape, 0) % LANES
    place = lax.broadcasted_iota(jnp.int32, spread_ref.shape, 1)
    column_of = (LANES // 2) * (place // LANES) + place % LANES // CCOL
    spread_ref[...] = jnp.where(column == column_of, 1.0, 0.0).astype(jnp.bfloat16)
    lane = lane_ids()
    start = lane // CCOL * CCOL
    next_lane = start + (lane + 1) % CCOL
    last_lane = start + (lane + CCOL - 1) % CCOL

    def tile(t):
        def load(level, variable):
            begin = (level + 1) * plane + variables * t + variable
            return flat_ref[pl.ds(begin, ROWS, stride=plane), :]

        changes = []
        winds = [
            (-CLOUD_ADVECT * TIME_STEP) * load(level, 3) for level in range(0, deep, ROWS)
        ]
        for variable in range(variables):
            for level in range(0, deep, ROWS):
                now = load(level, variable)
                ahead = pick(now, next_lane)
                behind = pick(now, last_lane)
                around = load(level - 1, variable) + load(level + 1, variable)
                change = winds[level // ROWS] * (ahead - behind) + (
                    CLOUD_DIFFUSE * TIME_STEP
                ) * (around - 2.0 * now)
                base = now + change
                base_ref[t, variable, level : level + ROWS, :] = base
                changes.append(RETAIN * base - now if variable == 2 else change)
        return changes

    def advance(step, carry):
        weights = pool_weights(step)
        pool_ref[step] = weights
        results = []
        for n in range(WIDE):
            if n % PIECE == 0:
                fetch((WIDE // PIECE) * step + n // PIECE).wait()
            results.append(tile(WIDE * step + n))
        sums[...] += pooled_sum(results, weights)
        return carry

    lax.fori_loop(0, steps, advance, 0)
    lower = lane_ids(deep) < LANES // 2
    for pair in range(2):
        mean_ref[pair] = jnp.where(
            lower,
            sums[deep * pair : deep * (pair + 1)],
            sums[deep * (2 + pair) : deep * (3 + pair)],
        )
    for copy in small:
        copy.wait()


def cloud_kernel(
    got_ref,
    base_ref,
    mean_ref,
    pool_ref,
    spread_ref,
    down_ref,
    up_ref,
    next_hbm,
    out_ref,
    forced,
    sums,
    next_ref,
    sem,
    whole,
):
    columns, variables, deep = base_ref.shape[:3]
    clev, levels = down_ref.shape
    plane = (columns + 1) * variables
    flat_ref = next_ref.reshape(clev * plane, LANES)
    steps = columns // WIDE
    half = LANES // 2
    fields = jnp.concatenate(gather_levels(got_ref, whole, levels), axis=1)
    forcing = jnp.dot(TIME_STEP * down_ref[...], fields, precision=EXACT)
    for pair in range(2):
        forced[pair, 0:clev] = forcing[:, LANES * pair : LANES * pair + LANES]
        forced[pair, clev:deep] = jnp.zeros((deep - clev, LANES), jnp.float32)
    sums[...] = jnp.zeros_like(sums)
    high, low = in_two(jnp.concatenate([forced[0], forced[1]], axis=0))

    def tile(t):
        shift = LANES - (LANES // CCOL) * t
        turned = [pltpu.roll(values, shift, 1) for values in (high, low)]
        push = jnp.dot(
            jnp.concatenate(turned, axis=1).astype(jnp.bfloat16),
            spread_ref[...],
            preferred_element_type=jnp.float32,
        )
        results = []
        for level in range(0, deep, ROWS):
            moved = []
            for variable in range(variables):
                begin = deep * (variable % 2) + level
                lanes = LANES * (variable // 2)
                moved.append(
                    base_ref[t, variable, level : level + ROWS, :]
                    + push[begin : begin + ROWS, lanes : lanes + LANES]
                )
            excess = moved[1] - SATURATION_BASE * jnp.exp2((SATURATION_SLOPE * LOG2_E) * moved[0])
            soft = jnp.maximum(excess, 0.0) + jnp.log(1.0 + jnp.exp2(-LOG2_E * jnp.abs(excess)))
            condensed = CONDENSE_RATE * soft
            updated = (
                moved[0] + condensed,
                moved[1] - condensed,
                RETAIN * moved[2] + condensed,
                moved[3],
            )
            count = min(ROWS, clev - level)
            for variable in range(variables):
                begin = level * plane + variables * t + variable
                flat_ref[pl.ds(begin, count, stride=plane), :] = updated[variable][:count]
            results.append(condensed)
        return results

    def store(begin, count):
        here = pl.ds(begin, count)
        return pltpu.make_async_copy(next_ref.at[:, here], next_hbm.at[:, here], sem)

    def advance(step, carry):
        results = []
        for n in range(WIDE):
            results.append(tile(WIDE * step + n))
            if (n + 1) % PIECE == 0:
                store(WIDE * step + n + 1 - PIECE, PIECE).start()
        sums[...] += pooled_sum(results, pool_ref[step])
        return carry

    lax.fori_loop(0, steps, advance, 0)
    lower = lane_ids(clev) < half
    extra = sums[0:clev]
    share = 1.0 / TIME_STEP
    first = mean_ref[0, 0:clev] + jnp.where(lower, share, share * RETAIN) * forced[0, 0:clev]
    first = first + extra
    second = mean_ref[1, 0:clev] + share * forced[1, 0:clev] - jnp.where(lower, extra, 0.0)
    feedback = lax.dot_general(
        up_ref[...],
        jnp.concatenate([first, second], axis=1),
        (((0,), (0,)), ((), ())),
        precision=EXACT,
    )
    scatter_levels(
        out_ref,
        far_row(whole),
        whole,
        [feedback[:, LANES * pair : LANES * pair + LANES] for pair in range(2)],
    )
    store(0, columns).wait()


def update_kernel(got_ref, partial_ref, out_ref, field, sorted_ref, whole, share):
    tiles = field.shape[0]
    rows = got_ref.shape[0] // (2 * tiles)
    unpack_pairs(got_ref, field)

    def collect(p):
        place = row_of(partial_ref[p, 1], order_row(whole)).astype(jnp.int32)
        for part, values in enumerate(reorder(field, p // 2 * 2, place)):
            sorted_ref[p, part] = values

    each(tiles, collect)
    swap_groups(sorted_ref, field, share)

    def finish(q):
        pack_pair(
            out_ref,
            q,
            rows,
            partial_ref[q, 0] + TIME_STEP * field[q, 0],
            partial_ref[q, 1] + TIME_STEP * field[q, 1],
        )

    each(tiles, finish)


def unpack_kernel(got_ref, state_ref, whole):
    elements, variables, nodes, levels = state_ref.shape
    for pair, by_level in enumerate(gather_levels(got_ref, whole, levels)):
        fields = by_level.T.reshape(2, elements, nodes, levels)
        state_ref[:, pair] = fields[0]
        state_ref[:, variables // 2 + pair] = fields[1]


def kernel_call(body, name, results, scratch, *operands, hbm_in=(), hbm_out=(), cost=None):
    spec = {True: pl.BlockSpec(memory_space=pltpu.HBM), False: pl.BlockSpec(memory_space=pltpu.VMEM)}
    operands = [
        pltpu.with_memory_space_constraint(value, pltpu.HBM) if n in hbm_in else value
        for n, value in enumerate(operands)
    ]
    return pl.pallas_call(
        body,
        name=name,
        out_shape=results,
        in_specs=[spec[n in hbm_in] for n in range(len(operands))],
        out_specs=tuple(spec[n in hbm_out] for n in range(len(results))),
        scratch_shapes=scratch,
        cost_estimate=cost,
        compiler_params=pltpu.CompilerParams(vmem_limit_bytes=KERNEL_VMEM),
    )(*operands)


def exchange(values, devices):
    slots = values.reshape(devices, values.shape[0] // devices, 1, LANES)
    moved = lax.all_to_all(slots, AXES, split_axis=0, concat_axis=0, tiled=True)
    return moved.reshape(values.shape)


def shards(
    model_state,
    cloud_state,
    neighbor,
    facing_edge,
    column_order,
    model_to_cloud_levels,
    cloud_to_model_levels,
):
    elements, variables, nodes, levels = model_state.shape
    clev, width = cloud_state.shape[1:]
    devices = lax.axis_size(AXES)
    block = column_order.shape[1]
    share = block // lax.axis_size("cols")
    whole = levels // devices
    left = levels - whole * devices
    assert variables == 4 and nodes == NODES and 2 * elements * nodes == LANES
    assert variables * left <= devices and left % ROWS == 0 and devices % ROWS == 0
    assert order_row(whole) < ROWS and block == 2 * LANES
    tiles = devices // 2
    f32 = jnp.float32
    shape = jax.ShapeDtypeStruct
    flat = shape((devices * (order_row(whole) + 1), LANES), f32)
    rows = shape((devices * far_row(whole), LANES), f32)
    pairs = shape((tiles, 2, ROWS, LANES), f32)
    columns = width // LANES
    assert columns % WIDE == 0 and WIDE % PIECE == 0
    deep = -(-clev // ROWS) * ROWS
    dma = pltpu.SemaphoreType.DMA

    packed, weights = kernel_call(
        functools.partial(pack_kernel, whole=whole, block=block),
        "pack_state",
        (flat, shape((2, LANES, 2 * LANES), jnp.bfloat16)),
        [
            pltpu.SMEM(neighbor.shape, jnp.int32),
            pltpu.SMEM(facing_edge.shape, jnp.int32),
            pltpu.VMEM(column_order.shape, jnp.int32),
            pltpu.VMEM(model_state.shape, f32),
            pltpu.VMEM((2, ROWS, block), f32),
            dma((5,)),
        ],
        neighbor,
        facing_edge,
        column_order,
        model_state,
        node_weights(),
        hbm_in=range(5),
    )
    by_level = exchange(packed, devices)
    arranged, partial = kernel_call(
        functools.partial(tendency_kernel, whole=whole, share=share),
        "tendency",
        (rows, pairs),
        [
            pltpu.VMEM(pairs.shape, f32),
            pltpu.VMEM((tiles, 2, ROWS, 2 * LANES), f32),
            pltpu.VMEM(pairs.shape, f32),
            pltpu.VMEM(pairs.shape, f32),
        ],
        by_level,
        weights,
    )
    by_tile = cloud_state.reshape(variables, clev, columns, LANES).transpose(1, 2, 0, 3)
    base, mean, pool, spread, down, up = kernel_call(
        settle_kernel,
        "settle",
        (
            shape((columns, variables, deep, LANES), f32),
            shape((2, deep, LANES), f32),
            shape((columns // WIDE, WIDE * LANES, LANES), jnp.bfloat16),
            shape((2 * LANES, 2 * LANES), jnp.bfloat16),
            shape((clev, levels), f32),
            shape((clev, levels), f32),
        ),
        [
            pltpu.VMEM((deep + 2, columns + 1, variables, LANES), f32),
            pltpu.VMEM((variables * deep, LANES), f32),
            dma((columns // PIECE + 2,)),
        ],
        by_tile,
        model_to_cloud_levels,
        cloud_to_model_levels.T,
        hbm_in=range(3),
        cost=pl.CostEstimate(flops=10**8, bytes_accessed=4 * 10**6, transcendentals=0),
    )
    by_column = exchange(arranged, devices)
    cloud_next, fed = kernel_call(
        functools.partial(cloud_kernel, whole=whole),
        "cloud",
        (shape(by_tile.shape, f32), rows),
        [
            pltpu.VMEM((2, deep, LANES), f32),
            pltpu.VMEM((deep, LANES), f32),
            pltpu.VMEM((clev, columns + 1, variables, LANES), f32),
            dma,
        ],
        by_column,
        base,
        mean,
        pool,
        spread,
        down,
        up,
        hbm_out=(0,),
    )
    fed_level = exchange(fed, devices)
    (advanced,) = kernel_call(
        functools.partial(update_kernel, whole=whole, share=share),
        "update",
        (rows,),
        [pltpu.VMEM(pairs.shape, f32), pltpu.VMEM(pairs.shape, f32)],
        fed_level,
        partial,
    )
    home = exchange(advanced, devices)
    (model_next,) = kernel_call(
        functools.partial(unpack_kernel, whole=whole),
        "unpack_state",
        (shape(model_state.shape, f32),),
        [],
        home,
    )
    cloud_next = cloud_next.transpose(2, 0, 1, 3).reshape(cloud_state.shape)
    return (model_next, cloud_next)


def solution(mesh):
    placed = (
        P(AXES, None, None, None),
        P(None, None, AXES),
        P(AXES, None),
        P(AXES, None),
        P("cols", None),
        P(),
        P(),
    )
    return jax.shard_map(
        shards,
        mesh=mesh,
        in_specs=placed,
        out_specs=(P(AXES, None, None, None), P(None, None, AXES)),
        check_vma=False,
    )
```

```python
import functools

import jax
import jax.numpy as jnp
import numpy as np
from jax import lax
from jax.experimental import pallas as pl
from jax.experimental.pallas import tpu as pltpu
from jax.sharding import PartitionSpec as P

CCOL = 32
NODES = 16
LANES = 128
ROWS = 8
AXES = ("cols", "vars")
VISCOSITY = 0.01
DRIFT = 0.05
PENALTY = 0.5
TIME_STEP = 0.5
CLOUD_ADVECT = 0.25
CLOUD_DIFFUSE = 0.1
CONDENSE_RATE = 0.3
SATURATION_BASE = 0.5
SATURATION_SLOPE = 0.3
RETAIN = 0.8
LOG2_E = 1.4426950408889634
EXACT = lax.Precision.HIGHEST
KERNEL_VMEM = 16 * 2**20
WIDE = 8
PIECE = 2
GROUP = 16
SWAPS = 4


def lobatto_derivative():
    points = np.array([-1.0, -1.0 / np.sqrt(5.0), 1.0 / np.sqrt(5.0), 1.0])
    derivative = np.zeros((4, 4))
    for target in range(4):
        for source in range(4):
            if target != source:
                weight_target = np.prod(
                    [points[target] - points[middle] for middle in range(4) if middle != target]
                )
                weight_source = np.prod(
                    [points[source] - points[middle] for middle in range(4) if middle != source]
                )
                derivative[target, source] = weight_target / (
                    weight_source * (points[target] - points[source])
                )
        derivative[target, target] = np.sum(
            [1.0 / (points[target] - points[middle]) for middle in range(4) if middle != target]
        )
    return derivative


def node_weights():
    derivative = lobatto_derivative()
    along_first = np.kron(np.eye(4), derivative)
    along_second = np.kron(derivative, np.eye(4))
    laplace = along_first @ along_first + along_second @ along_second
    edges = np.zeros((4, 4))
    edges[0, :] += 1.0
    edges[3, :] += 1.0
    edges[:, 0] += 1.0
    edges[:, 3] += 1.0
    linear = VISCOSITY * laplace - PENALTY * np.diag(edges.reshape(-1))
    repeat = np.eye(LANES // NODES)
    weights = np.concatenate(
        [np.kron(repeat, linear.T), np.kron(repeat, -DRIFT * along_first.T)], axis=1
    )
    high = weights.astype(jnp.bfloat16)
    low = (weights - high.astype(np.float64)).astype(jnp.bfloat16)
    return jnp.asarray(np.stack([high, low]))


def each(count, body, group=GROUP):
    group = min(group, count)
    if count <= group:
        for index in range(count):
            body(index)
        return

    def several(first, carry):
        for n in range(group):
            body(first * group + n)
        return carry

    lax.fori_loop(0, count // group, several, 0)


def lane_ids(rows=ROWS):
    return lax.broadcasted_iota(jnp.int32, (rows, LANES), 1)


def row_ids():
    return lax.broadcasted_iota(jnp.int32, (ROWS, LANES), 0)


def pick(values, lanes):
    return jnp.take_along_axis(values, lanes, axis=1, mode="promise_in_bounds")


def half_turn(values):
    return pltpu.roll(values, LANES // 2, 1)


def slot_rows(slot, rows):
    return pl.ds(slot * rows, rows)


def split_pair(first, second):
    lower = lane_ids(first.shape[0]) < LANES // 2
    return (
        jnp.where(lower, first, half_turn(second)),
        jnp.where(lower, half_turn(first), second),
    )


def row_of(values, row):
    return jnp.broadcast_to(values[row : row + 1], (ROWS, LANES))


def far_row(whole):
    return 2 * whole + 1


def order_row(whole):
    return 2 * whole + 2


def scatter_levels(out_ref, pitch, whole, parts, with_wind=False):
    devices = out_ref.shape[0] // pitch
    levels = parts[0].shape[0]
    for pair in range(2):
        for turn in range(whole):
            for first in range(0, devices, ROWS):
                begin = turn * devices + first
                out_ref[pl.ds(pitch * first + 2 * turn + pair, ROWS, stride=pitch), :] = parts[
                    pair
                ][begin : begin + ROWS]
    for first in range(whole * devices, levels, ROWS):
        wind = parts[1][first : first + ROWS]
        for variable in range(4):
            values = parts[variable % 2][first : first + ROWS]
            if variable >= 2:
                values = half_turn(values)
            if with_wind:
                values = jnp.where(lane_ids() < LANES // 2, values, wind)
            begin = pitch * (4 * (first - whole * devices) + variable) + 2 * whole
            out_ref[pl.ds(begin, ROWS, stride=4 * pitch), :] = values


def gather_levels(got_ref, whole, levels):
    pitch = 2 * whole + 1
    devices = got_ref.shape[0] // pitch
    parts = []
    for pair in range(2):
        pieces = [
            got_ref[pl.ds(pitch * first + 2 * turn + pair, ROWS, stride=pitch), :]
            for turn in range(whole)
            for first in range(0, devices, ROWS)
        ]
        for first in range(whole * devices, levels, ROWS):
            lower, upper = (
                got_ref[
                    pl.ds(
                        pitch * (4 * (first - whole * devices) + variable) + 2 * whole,
                        ROWS,
                        stride=4 * pitch,
                    ),
                    :,
                ]
                for variable in (pair, 2 + pair)
            )
            pieces.append(jnp.where(lane_ids() < LANES // 2, lower, half_turn(upper)))
        parts.append(jnp.concatenate(pieces, axis=0))
    return parts


def unpack_pairs(got_ref, field):
    rows = got_ref.shape[0] // (2 * field.shape[0])

    def unpack(q):
        low, high = split_pair(
            got_ref[slot_rows(2 * q, rows), :], got_ref[slot_rows(2 * q + 1, rows), :]
        )
        field[q, 0, :rows] = low
        field[q, 1, :rows] = high

    each(field.shape[0], unpack)


def pack_pair(out_ref, q, rows, low, high):
    first, second = split_pair(low, high)
    out_ref[slot_rows(2 * q, rows), :] = first[:rows]
    out_ref[slot_rows(2 * q + 1, rows), :] = second[:rows]


def swap_groups(source, target, share):
    groups = LANES // share
    group = lane_ids() // share

    def swap(index):
        x = index // 2
        y = index % 2

        def gather(w):
            for part in range(2):
                joined = source[2 * groups * x + y, part]
                joined = pltpu.roll(joined, (LANES - share * w) % LANES, 1)
                for u in range(1, groups):
                    other = source[2 * (groups * x + u) + y, part]
                    turned = pltpu.roll(other, (share * (u + groups - w)) % LANES, 1)
                    joined = jnp.where(group == u, turned, joined)
                target[2 * (groups * y + w) + x, part] = joined

        each(groups, gather)

    each(4, swap, SWAPS)


def reorder(source, block_tile, places):
    spot = places & (LANES - 1)
    first = places < LANES
    return [
        jnp.where(
            first,
            pick(source[block_tile, part], spot),
            pick(source[block_tile + 1, part], spot),
        )
        for part in range(2)
    ]


def pack_kernel(
    nbr_hbm,
    face_hbm,
    order_hbm,
    state_hbm,
    weight_hbm,
    out_ref,
    weight_ref,
    nbr_ref,
    face_ref,
    order_ref,
    state_ref,
    scratch,
    sems,
    whole,
    block,
):
    copies = [
        pltpu.make_async_copy(source, target, sems.at[n])
        for n, (source, target) in enumerate(
            (
                (nbr_hbm, nbr_ref),
                (face_hbm, face_ref),
                (order_hbm, order_ref),
                (state_hbm, state_ref),
                (weight_hbm, weight_ref),
            )
        )
    ]
    for copy in copies:
        copy.start()
    elements, variables, nodes, levels = state_ref.shape
    half = LANES // 2
    lane = lane_ids()
    own = lax.axis_index("vars")
    column = lane % half
    elem = column // nodes
    along_y = (column // 4) % 4
    along_x = column % 4
    upper = lane >= half
    edge = jnp.where(
        upper,
        jnp.where(along_x == 3, 1, jnp.where(along_x == 0, 3, -1)),
        jnp.where(along_y == 0, 0, jnp.where(along_y == 3, 2, -1)),
    )
    along = jnp.where(upper, along_y, along_x)
    place = jnp.where(edge >= 2, 3 - along, along)
    out_ref[...] = jnp.zeros_like(out_ref)
    copies[0].wait()
    copies[1].wait()
    far = jnp.zeros_like(lane)
    face = jnp.zeros_like(lane)
    for e in range(elements):
        for j in range(4):
            here = (elem == e) & (edge == j)
            far = jnp.where(here, nbr_ref[e, j], far)
            face = jnp.where(here, face_ref[e, j], face)
    node = jnp.where(
        face == 0,
        3 - place,
        jnp.where(face == 1, 15 - 4 * place, jnp.where(face == 2, 12 + place, 4 * place)),
    )
    far_col = jnp.where(edge >= 0, nodes * far + node, -1).astype(jnp.float32)

    copies[2].wait()
    order = order_ref[...]
    spots = lax.broadcasted_iota(jnp.int32, (block, block), 0)
    marks = (spots == order).astype(jnp.float32).astype(jnp.bfloat16)
    numbers = lax.broadcasted_iota(jnp.int32, (ROWS, block), 1).astype(jnp.float32)
    scratch[0] = jnp.broadcast_to(order, (ROWS, block)).astype(jnp.float32)
    scratch[1] = lax.dot_general(
        numbers.astype(jnp.bfloat16),
        marks,
        (((1,), (1,)), ((), ())),
        preferred_element_type=jnp.float32,
    )
    begin = pl.multiple_of((own // 2) * LANES, LANES)
    order_part = scratch[0, :, pl.ds(begin, LANES)]
    place_part = scratch[1, :, pl.ds(begin, LANES)]
    odd = own % 2 == 1
    order_part = jnp.where(odd, half_turn(order_part), order_part)
    place_part = jnp.where(odd, place_part, half_turn(place_part))
    indices = jnp.where(upper, place_part, order_part)

    pitch = order_row(whole) + 1
    slots = out_ref.shape[0] // pitch
    for first in range(0, slots, ROWS):
        out_ref[pl.ds(pitch * first + far_row(whole), ROWS, stride=pitch), :] = far_col
        out_ref[pl.ds(pitch * first + order_row(whole), ROWS, stride=pitch), :] = indices
    copies[3].wait()
    parts = []
    for pair in range(variables // 2):
        fields = jnp.concatenate(
            [
                state_ref[:, pair].reshape(elements * nodes, levels),
                state_ref[:, variables // 2 + pair].reshape(elements * nodes, levels),
            ],
            axis=0,
        )
        parts.append(fields.T)
    scatter_levels(out_ref, pitch, whole, parts, with_wind=True)
    copies[4].wait()


def tendency_kernel(
    got_ref,
    weight_ref,
    settled_ref,
    out_ref,
    partial_ref,
    field,
    linear,
    tend,
    moved,
    whole,
    share,
):
    tiles = field.shape[0]
    row = row_ids()
    lower = lane_ids() < LANES // 2
    wind_row = jnp.where(row < 2 * whole, row | 1, 2 * whole)
    unpack_pairs(got_ref, field)
    step = min(tiles, 16)

    def multiply(chunk):
        fields = field[pl.ds(chunk * step, step)].reshape(step * 2 * ROWS, LANES)
        high, low = in_two(fields)
        coarse, fine = weight_ref[0], weight_ref[1]
        result = jnp.dot(
            jnp.concatenate([high, low], axis=1),
            jnp.concatenate([coarse, coarse], axis=0),
            preferred_element_type=jnp.float32,
        ) + jnp.dot(high, fine, preferred_element_type=jnp.float32)
        linear[pl.ds(chunk * step, step)] = result.reshape(step, 2, ROWS, 2 * LANES)

    each(tiles // step, multiply, 1)

    def advance(q):
        before = jnp.where(q == 0, tiles - 1, q - 1)
        after = jnp.where(q == tiles - 1, 0, q + 1)
        high = field[q, 1]
        wind = jnp.take_along_axis(high, wind_row, axis=0, mode="promise_in_bounds")
        sums = [0.0, 0.0]
        for side in range(2):
            far = row_of(field[q, side], far_row(whole)).astype(jnp.int32)
            spot = far & (LANES - 1)
            inside = lax.shift_right_arithmetic(far, 7) == q
            for part in range(2):
                beside = jnp.where(lower, field[after, part], field[before, part])
                value = jnp.where(inside, pick(field[q, part], spot), pick(beside, spot))
                sums[part] = sums[part] + jnp.where(far >= 0, value, 0.0)
        for part in range(2):
            own = field[q, part]
            result = (
                linear[q, part, :, :LANES]
                + wind * linear[q, part, :, LANES:]
                + PENALTY * sums[part]
            )
            tend[q, part] = result
            partial_ref[q, part] = jnp.where(
                row < far_row(whole), own + TIME_STEP * result, own
            )

    each(tiles, advance)
    swap_groups(tend, moved, share)

    def arrange(p):
        order = row_of(field[p, 0], order_row(whole)).astype(jnp.int32)
        pack_pair(out_ref, p, far_row(whole), *reorder(moved, p // 2 * 2, order))

    each(tiles, arrange)


def in_two(values):
    high = values.astype(jnp.bfloat16)
    low = (values - high.astype(jnp.float32)).astype(jnp.bfloat16)
    return high, low


def pool_weights(step):
    wide = WIDE * LANES
    lane = lax.broadcasted_iota(jnp.int32, (wide, LANES), 1) % (LANES // 2)
    owner = lax.broadcasted_iota(jnp.int32, (wide, LANES), 0) // CCOL
    mean = 1.0 / (CCOL * TIME_STEP)
    return jnp.where(lane == (wide // CCOL) * step + owner, mean, 0.0).astype(jnp.bfloat16)


def pooled_sum(tiles, weights):
    joined = jnp.concatenate([jnp.concatenate(tile, axis=0) for tile in tiles], axis=1)
    rows = joined.shape[0]
    both = jnp.concatenate(in_two(joined), axis=0)
    result = jnp.dot(both, weights, preferred_element_type=jnp.float32)
    return result[:rows] + result[rows:]


def settle_kernel(
    cloud_hbm,
    down_hbm,
    up_hbm,
    base_ref,
    mean_ref,
    pool_ref,
    spread_ref,
    down_ref,
    up_ref,
    cloud_ref,
    sums,
    sems,
):
    columns, variables, deep = base_ref.shape[:3]
    clev = cloud_hbm.shape[0]
    plane = (columns + 1) * variables
    steps = columns // WIDE
    small = [
        pltpu.make_async_copy(down_hbm, down_ref, sems.at[columns // PIECE]),
        pltpu.make_async_copy(up_hbm, up_ref, sems.at[columns // PIECE + 1]),
    ]

    def fetch(step):
        here = pl.ds(PIECE * step, PIECE)
        return pltpu.make_async_copy(
            cloud_hbm.at[:, here], cloud_ref.at[pl.ds(1, clev), here], sems.at[step]
        )

    pieces = columns // PIECE
    for step in range(pieces):
        fetch(step).start()
    for copy in small:
        copy.start()
    flat_ref = cloud_ref.reshape((deep + 2) * plane, LANES)
    rim = jnp.zeros((plane, LANES), jnp.float32)
    flat_ref[0:plane] = rim
    for level in range(clev, deep + 1):
        flat_ref[(level + 1) * plane : (level + 2) * plane] = rim
    sums[...] = jnp.zeros_like(sums)
    column = lax.broadcasted_iota(jnp.int32, spread_ref.shape, 0) % LANES
    place = lax.broadcasted_iota(jnp.int32, spread_ref.shape, 1)
    column_of = (LANES // 2) * (place // LANES) + place % LANES // CCOL
    spread_ref[...] = jnp.where(column == column_of, 1.0, 0.0).astype(jnp.bfloat16)
    lane = lane_ids()
    start = lane // CCOL * CCOL
    next_lane = start + (lane + 1) % CCOL
    last_lane = start + (lane + CCOL - 1) % CCOL

    def tile(t):
        def load(level, variable):
            begin = (level + 1) * plane + variables * t + variable
            return flat_ref[pl.ds(begin, ROWS, stride=plane), :]

        changes = []
        winds = [
            (-CLOUD_ADVECT * TIME_STEP) * load(level, 3) for level in range(0, deep, ROWS)
        ]
        for variable in range(variables):
            for level in range(0, deep, ROWS):
                now = load(level, variable)
                ahead = pick(now, next_lane)
                behind = pick(now, last_lane)
                around = load(level - 1, variable) + load(level + 1, variable)
                change = winds[level // ROWS] * (ahead - behind) + (
                    CLOUD_DIFFUSE * TIME_STEP
                ) * (around - 2.0 * now)
                base = now + change
                base_ref[t, variable, level : level + ROWS, :] = base
                changes.append(RETAIN * base - now if variable == 2 else change)
        return changes

    def advance(step, carry):
        weights = pool_weights(step)
        pool_ref[step] = weights
        results = []
        for n in range(WIDE):
            if n % PIECE == 0:
                fetch((WIDE // PIECE) * step + n // PIECE).wait()
            results.append(tile(WIDE * step + n))
        sums[...] += pooled_sum(results, weights)
        return carry

    lax.fori_loop(0, steps, advance, 0)
    lower = lane_ids(deep) < LANES // 2
    for pair in range(2):
        mean_ref[pair] = jnp.where(
            lower,
            sums[deep * pair : deep * (pair + 1)],
            sums[deep * (2 + pair) : deep * (3 + pair)],
        )
    for copy in small:
        copy.wait()


def cloud_kernel(
    got_ref,
    base_ref,
    mean_ref,
    pool_ref,
    spread_ref,
    down_ref,
    up_ref,
    next_hbm,
    out_ref,
    forced,
    sums,
    next_ref,
    sem,
    whole,
):
    columns, variables, deep = base_ref.shape[:3]
    clev, levels = down_ref.shape
    plane = (columns + 1) * variables
    flat_ref = next_ref.reshape(clev * plane, LANES)
    steps = columns // WIDE
    half = LANES // 2
    fields = jnp.concatenate(gather_levels(got_ref, whole, levels), axis=1)
    forcing = jnp.dot(TIME_STEP * down_ref[...], fields, precision=EXACT)
    for pair in range(2):
        forced[pair, 0:clev] = forcing[:, LANES * pair : LANES * pair + LANES]
        forced[pair, clev:deep] = jnp.zeros((deep - clev, LANES), jnp.float32)
    sums[...] = jnp.zeros_like(sums)
    high, low = in_two(jnp.concatenate([forced[0], forced[1]], axis=0))

    def tile(t):
        shift = LANES - (LANES // CCOL) * t
        turned = [pltpu.roll(values, shift, 1) for values in (high, low)]
        push = jnp.dot(
            jnp.concatenate(turned, axis=1).astype(jnp.bfloat16),
            spread_ref[...],
            preferred_element_type=jnp.float32,
        )
        results = []
        for level in range(0, deep, ROWS):
            moved = []
            for variable in range(variables):
                begin = deep * (variable % 2) + level
                lanes = LANES * (variable // 2)
                moved.append(
                    base_ref[t, variable, level : level + ROWS, :]
                    + push[begin : begin + ROWS, lanes : lanes + LANES]
                )
            excess = moved[1] - SATURATION_BASE * jnp.exp2((SATURATION_SLOPE * LOG2_E) * moved[0])
            soft = jnp.maximum(excess, 0.0) + jnp.log(1.0 + jnp.exp2(-LOG2_E * jnp.abs(excess)))
            condensed = CONDENSE_RATE * soft
            updated = (
                moved[0] + condensed,
                moved[1] - condensed,
                RETAIN * moved[2] + condensed,
                moved[3],
            )
            count = min(ROWS, clev - level)
            for variable in range(variables):
                begin = level * plane + variables * t + variable
                flat_ref[pl.ds(begin, count, stride=plane), :] = updated[variable][:count]
            results.append(condensed)
        return results

    def store(begin, count):
        here = pl.ds(begin, count)
        return pltpu.make_async_copy(next_ref.at[:, here], next_hbm.at[:, here], sem)

    def advance(step, carry):
        results = []
        for n in range(WIDE):
            results.append(tile(WIDE * step + n))
            if (n + 1) % PIECE == 0:
                store(WIDE * step + n + 1 - PIECE, PIECE).start()
        sums[...] += pooled_sum(results, pool_ref[step])
        return carry

    lax.fori_loop(0, steps, advance, 0)
    lower = lane_ids(clev) < half
    extra = sums[0:clev]
    share = 1.0 / TIME_STEP
    first = mean_ref[0, 0:clev] + jnp.where(lower, share, share * RETAIN) * forced[0, 0:clev]
    first = first + extra
    second = mean_ref[1, 0:clev] + share * forced[1, 0:clev] - jnp.where(lower, extra, 0.0)
    feedback = lax.dot_general(
        up_ref[...],
        jnp.concatenate([first, second], axis=1),
        (((0,), (0,)), ((), ())),
        precision=EXACT,
    )
    scatter_levels(
        out_ref,
        far_row(whole),
        whole,
        [feedback[:, LANES * pair : LANES * pair + LANES] for pair in range(2)],
    )
    store(0, columns).wait()


def update_kernel(got_ref, partial_ref, out_ref, field, sorted_ref, whole, share):
    tiles = field.shape[0]
    rows = got_ref.shape[0] // (2 * tiles)
    unpack_pairs(got_ref, field)

    def collect(p):
        place = row_of(partial_ref[p, 1], order_row(whole)).astype(jnp.int32)
        for part, values in enumerate(reorder(field, p // 2 * 2, place)):
            sorted_ref[p, part] = values

    each(tiles, collect)
    swap_groups(sorted_ref, field, share)

    def finish(q):
        pack_pair(
            out_ref,
            q,
            rows,
            partial_ref[q, 0] + TIME_STEP * field[q, 0],
            partial_ref[q, 1] + TIME_STEP * field[q, 1],
        )

    each(tiles, finish)


def unpack_kernel(got_ref, state_ref, whole):
    elements, variables, nodes, levels = state_ref.shape
    for pair, by_level in enumerate(gather_levels(got_ref, whole, levels)):
        fields = by_level.T.reshape(2, elements, nodes, levels)
        state_ref[:, pair] = fields[0]
        state_ref[:, variables // 2 + pair] = fields[1]


def kernel_call(body, name, results, scratch, *operands, hbm_in=(), hbm_out=(), cost=None):
    spec = {True: pl.BlockSpec(memory_space=pltpu.HBM), False: pl.BlockSpec(memory_space=pltpu.VMEM)}
    operands = [
        pltpu.with_memory_space_constraint(value, pltpu.HBM) if n in hbm_in else value
        for n, value in enumerate(operands)
    ]
    return pl.pallas_call(
        body,
        name=name,
        out_shape=results,
        in_specs=[spec[n in hbm_in] for n in range(len(operands))],
        out_specs=tuple(spec[n in hbm_out] for n in range(len(results))),
        scratch_shapes=scratch,
        cost_estimate=cost,
        compiler_params=pltpu.CompilerParams(vmem_limit_bytes=KERNEL_VMEM),
    )(*operands)


def exchange(values, devices):
    slots = values.reshape(devices, values.shape[0] // devices, 1, LANES)
    moved = lax.all_to_all(slots, AXES, split_axis=0, concat_axis=0, tiled=True)
    return moved.reshape(values.shape)


def shards(
    model_state,
    cloud_state,
    neighbor,
    facing_edge,
    column_order,
    model_to_cloud_levels,
    cloud_to_model_levels,
):
    elements, variables, nodes, levels = model_state.shape
    clev, width = cloud_state.shape[1:]
    devices = lax.axis_size(AXES)
    block = column_order.shape[1]
    share = block // lax.axis_size("cols")
    whole = levels // devices
    left = levels - whole * devices
    assert variables == 4 and nodes == NODES and 2 * elements * nodes == LANES
    assert variables * left <= devices and left % ROWS == 0 and devices % ROWS == 0
    assert order_row(whole) < ROWS and block == 2 * LANES
    tiles = devices // 2
    f32 = jnp.float32
    shape = jax.ShapeDtypeStruct
    flat = shape((devices * (order_row(whole) + 1), LANES), f32)
    rows = shape((devices * far_row(whole), LANES), f32)
    pairs = shape((tiles, 2, ROWS, LANES), f32)
    columns = width // LANES
    assert columns % WIDE == 0 and WIDE % PIECE == 0
    deep = -(-clev // ROWS) * ROWS
    dma = pltpu.SemaphoreType.DMA

    packed, weights = kernel_call(
        functools.partial(pack_kernel, whole=whole, block=block),
        "pack_state",
        (flat, shape((2, LANES, 2 * LANES), jnp.bfloat16)),
        [
            pltpu.SMEM(neighbor.shape, jnp.int32),
            pltpu.SMEM(facing_edge.shape, jnp.int32),
            pltpu.VMEM(column_order.shape, jnp.int32),
            pltpu.VMEM(model_state.shape, f32),
            pltpu.VMEM((2, ROWS, block), f32),
            dma((5,)),
        ],
        neighbor,
        facing_edge,
        column_order,
        model_state,
        node_weights(),
        hbm_in=range(5),
    )
    by_level = exchange(packed, devices)
    by_tile = cloud_state.reshape(variables, clev, columns, LANES).transpose(1, 2, 0, 3)
    base, mean, pool, spread, down, up = kernel_call(
        settle_kernel,
        "settle",
        (
            shape((columns, variables, deep, LANES), f32),
            shape((2, deep, LANES), f32),
            shape((columns // WIDE, WIDE * LANES, LANES), jnp.bfloat16),
            shape((2 * LANES, 2 * LANES), jnp.bfloat16),
            shape((clev, levels), f32),
            shape((clev, levels), f32),
        ),
        [
            pltpu.VMEM((deep + 2, columns + 1, variables, LANES), f32),
            pltpu.VMEM((variables * deep, LANES), f32),
            dma((columns // PIECE + 2,)),
        ],
        by_tile,
        model_to_cloud_levels,
        cloud_to_model_levels.T,
        hbm_in=range(3),
        cost=pl.CostEstimate(flops=10**8, bytes_accessed=4 * 10**6, transcendentals=0),
    )
    arranged, partial = kernel_call(
        functools.partial(tendency_kernel, whole=whole, share=share),
        "tendency",
        (rows, pairs),
        [
            pltpu.VMEM(pairs.shape, f32),
            pltpu.VMEM((tiles, 2, ROWS, 2 * LANES), f32),
            pltpu.VMEM(pairs.shape, f32),
            pltpu.VMEM(pairs.shape, f32),
        ],
        by_level,
        weights,
        down,
    )
    by_column = exchange(arranged, devices)
    cloud_next, fed = kernel_call(
        functools.partial(cloud_kernel, whole=whole),
        "cloud",
        (shape(by_tile.shape, f32), rows),
        [
            pltpu.VMEM((2, deep, LANES), f32),
            pltpu.VMEM((deep, LANES), f32),
            pltpu.VMEM((clev, columns + 1, variables, LANES), f32),
            dma,
        ],
        by_column,
        base,
        mean,
        pool,
        spread,
        down,
        up,
        hbm_out=(0,),
    )
    fed_level = exchange(fed, devices)
    (advanced,) = kernel_call(
        functools.partial(update_kernel, whole=whole, share=share),
        "update",
        (rows,),
        [pltpu.VMEM(pairs.shape, f32), pltpu.VMEM(pairs.shape, f32)],
        fed_level,
        partial,
    )
    home = exchange(advanced, devices)
    (model_next,) = kernel_call(
        functools.partial(unpack_kernel, whole=whole),
        "unpack_state",
        (shape(model_state.shape, f32),),
        [],
        home,
    )
    cloud_next = cloud_next.transpose(2, 0, 1, 3).reshape(cloud_state.shape)
    return (model_next, cloud_next)


def solution(mesh):
    placed = (
        P(AXES, None, None, None),
        P(None, None, AXES),
        P(AXES, None),
        P(AXES, None),
        P("cols", None),
        P(),
        P(),
    )
    return jax.shard_map(
        shards,
        mesh=mesh,
        in_specs=placed,
        out_specs=(P(AXES, None, None, None), P(None, None, AXES)),
        check_vma=False,
    )
```

```python
import functools

import jax
import jax.numpy as jnp
import numpy as np
from jax import lax
from jax.experimental import pallas as pl
from jax.experimental.pallas import tpu as pltpu
from jax.sharding import PartitionSpec as P

CCOL = 32
NODES = 16
LANES = 128
ROWS = 8
AXES = ("cols", "vars")
VISCOSITY = 0.01
DRIFT = 0.05
PENALTY = 0.5
TIME_STEP = 0.5
CLOUD_ADVECT = 0.25
CLOUD_DIFFUSE = 0.1
CONDENSE_RATE = 0.3
SATURATION_BASE = 0.5
SATURATION_SLOPE = 0.3
RETAIN = 0.8
LOG2_E = 1.4426950408889634
EXACT = lax.Precision.HIGHEST
KERNEL_VMEM = 16 * 2**20
WIDE = 16
PIECE = 2
GROUP = 16
SWAPS = 4


def lobatto_derivative():
    points = np.array([-1.0, -1.0 / np.sqrt(5.0), 1.0 / np.sqrt(5.0), 1.0])
    derivative = np.zeros((4, 4))
    for target in range(4):
        for source in range(4):
            if target != source:
                weight_target = np.prod(
                    [points[target] - points[middle] for middle in range(4) if middle != target]
                )
                weight_source = np.prod(
                    [points[source] - points[middle] for middle in range(4) if middle != source]
                )
                derivative[target, source] = weight_target / (
                    weight_source * (points[target] - points[source])
                )
        derivative[target, target] = np.sum(
            [1.0 / (points[target] - points[middle]) for middle in range(4) if middle != target]
        )
    return derivative


def node_weights():
    derivative = lobatto_derivative()
    along_first = np.kron(np.eye(4), derivative)
    along_second = np.kron(derivative, np.eye(4))
    laplace = along_first @ along_first + along_second @ along_second
    edges = np.zeros((4, 4))
    edges[0, :] += 1.0
    edges[3, :] += 1.0
    edges[:, 0] += 1.0
    edges[:, 3] += 1.0
    linear = VISCOSITY * laplace - PENALTY * np.diag(edges.reshape(-1))
    repeat = np.eye(LANES // NODES)
    weights = np.concatenate(
        [np.kron(repeat, linear.T), np.kron(repeat, -DRIFT * along_first.T)], axis=1
    )
    high = weights.astype(jnp.bfloat16)
    low = (weights - high.astype(np.float64)).astype(jnp.bfloat16)
    return jnp.asarray(np.stack([high, low]))


def each(count, body, group=GROUP):
    group = min(group, count)
    if count <= group:
        for index in range(count):
            body(index)
        return

    def several(first, carry):
        for n in range(group):
            body(first * group + n)
        return carry

    lax.fori_loop(0, count // group, several, 0)


def lane_ids(rows=ROWS):
    return lax.broadcasted_iota(jnp.int32, (rows, LANES), 1)


def row_ids():
    return lax.broadcasted_iota(jnp.int32, (ROWS, LANES), 0)


def pick(values, lanes):
    return jnp.take_along_axis(values, lanes, axis=1, mode="promise_in_bounds")


def half_turn(values):
    return pltpu.roll(values, LANES // 2, 1)


def slot_rows(slot, rows):
    return pl.ds(slot * rows, rows)


def split_pair(first, second):
    lower = lane_ids(first.shape[0]) < LANES // 2
    return (
        jnp.where(lower, first, half_turn(second)),
        jnp.where(lower, half_turn(first), second),
    )


def row_of(values, row):
    return jnp.broadcast_to(values[row : row + 1], (ROWS, LANES))


def far_row(whole):
    return 2 * whole + 1


def order_row(whole):
    return 2 * whole + 2


def scatter_levels(out_ref, pitch, whole, parts, with_wind=False):
    devices = out_ref.shape[0] // pitch
    levels = parts[0].shape[0]
    for pair in range(2):
        for turn in range(whole):
            for first in range(0, devices, ROWS):
                begin = turn * devices + first
                out_ref[pl.ds(pitch * first + 2 * turn + pair, ROWS, stride=pitch), :] = parts[
                    pair
                ][begin : begin + ROWS]
    for first in range(whole * devices, levels, ROWS):
        wind = parts[1][first : first + ROWS]
        for variable in range(4):
            values = parts[variable % 2][first : first + ROWS]
            if variable >= 2:
                values = half_turn(values)
            if with_wind:
                values = jnp.where(lane_ids() < LANES // 2, values, wind)
            begin = pitch * (4 * (first - whole * devices) + variable) + 2 * whole
            out_ref[pl.ds(begin, ROWS, stride=4 * pitch), :] = values


def gather_levels(got_ref, whole, levels):
    pitch = 2 * whole + 1
    devices = got_ref.shape[0] // pitch
    parts = []
    for pair in range(2):
        pieces = [
            got_ref[pl.ds(pitch * first + 2 * turn + pair, ROWS, stride=pitch), :]
            for turn in range(whole)
            for first in range(0, devices, ROWS)
        ]
        for first in range(whole * devices, levels, ROWS):
            lower, upper = (
                got_ref[
                    pl.ds(
                        pitch * (4 * (first - whole * devices) + variable) + 2 * whole,
                        ROWS,
                        stride=4 * pitch,
                    ),
                    :,
                ]
                for variable in (pair, 2 + pair)
            )
            pieces.append(jnp.where(lane_ids() < LANES // 2, lower, half_turn(upper)))
        parts.append(jnp.concatenate(pieces, axis=0))
    return parts


def unpack_pairs(got_ref, field):
    rows = got_ref.shape[0] // (2 * field.shape[0])

    def unpack(q):
        low, high = split_pair(
            got_ref[slot_rows(2 * q, rows), :], got_ref[slot_rows(2 * q + 1, rows), :]
        )
        field[q, 0, :rows] = low
        field[q, 1, :rows] = high

    each(field.shape[0], unpack)


def pack_pair(out_ref, q, rows, low, high):
    first, second = split_pair(low, high)
    out_ref[slot_rows(2 * q, rows), :] = first[:rows]
    out_ref[slot_rows(2 * q + 1, rows), :] = second[:rows]


def swap_groups(source, target, share):
    groups = LANES // share
    group = lane_ids() // share

    def swap(index):
        x = index // 2
        y = index % 2

        def gather(w):
            for part in range(2):
                joined = source[2 * groups * x + y, part]
                joined = pltpu.roll(joined, (LANES - share * w) % LANES, 1)
                for u in range(1, groups):
                    other = source[2 * (groups * x + u) + y, part]
                    turned = pltpu.roll(other, (share * (u + groups - w)) % LANES, 1)
                    joined = jnp.where(group == u, turned, joined)
                target[2 * (groups * y + w) + x, part] = joined

        each(groups, gather)

    each(4, swap, SWAPS)


def reorder(source, block_tile, places):
    spot = places & (LANES - 1)
    first = places < LANES
    return [
        jnp.where(
            first,
            pick(source[block_tile, part], spot),
            pick(source[block_tile + 1, part], spot),
        )
        for part in range(2)
    ]


def pack_kernel(
    nbr_hbm,
    face_hbm,
    order_hbm,
    state_hbm,
    weight_hbm,
    out_ref,
    weight_ref,
    nbr_ref,
    face_ref,
    order_ref,
    state_ref,
    scratch,
    sems,
    whole,
    block,
):
    copies = [
        pltpu.make_async_copy(source, target, sems.at[n])
        for n, (source, target) in enumerate(
            (
                (nbr_hbm, nbr_ref),
                (face_hbm, face_ref),
                (order_hbm, order_ref),
                (state_hbm, state_ref),
                (weight_hbm, weight_ref),
            )
        )
    ]
    for copy in copies:
        copy.start()
    elements, variables, nodes, levels = state_ref.shape
    half = LANES // 2
    lane = lane_ids()
    own = lax.axis_index("vars")
    column = lane % half
    elem = column // nodes
    along_y = (column // 4) % 4
    along_x = column % 4
    upper = lane >= half
    edge = jnp.where(
        upper,
        jnp.where(along_x == 3, 1, jnp.where(along_x == 0, 3, -1)),
        jnp.where(along_y == 0, 0, jnp.where(along_y == 3, 2, -1)),
    )
    along = jnp.where(upper, along_y, along_x)
    place = jnp.where(edge >= 2, 3 - along, along)
    out_ref[...] = jnp.zeros_like(out_ref)
    copies[0].wait()
    copies[1].wait()
    far = jnp.zeros_like(lane)
    face = jnp.zeros_like(lane)
    for e in range(elements):
        for j in range(4):
            here = (elem == e) & (edge == j)
            far = jnp.where(here, nbr_ref[e, j], far)
            face = jnp.where(here, face_ref[e, j], face)
    node = jnp.where(
        face == 0,
        3 - place,
        jnp.where(face == 1, 15 - 4 * place, jnp.where(face == 2, 12 + place, 4 * place)),
    )
    far_col = jnp.where(edge >= 0, nodes * far + node, -1).astype(jnp.float32)

    copies[2].wait()
    order = order_ref[...]
    spots = lax.broadcasted_iota(jnp.int32, (block, block), 0)
    marks = (spots == order).astype(jnp.float32).astype(jnp.bfloat16)
    numbers = lax.broadcasted_iota(jnp.int32, (ROWS, block), 1).astype(jnp.float32)
    scratch[0] = jnp.broadcast_to(order, (ROWS, block)).astype(jnp.float32)
    scratch[1] = lax.dot_general(
        numbers.astype(jnp.bfloat16),
        marks,
        (((1,), (1,)), ((), ())),
        preferred_element_type=jnp.float32,
    )
    begin = pl.multiple_of((own // 2) * LANES, LANES)
    order_part = scratch[0, :, pl.ds(begin, LANES)]
    place_part = scratch[1, :, pl.ds(begin, LANES)]
    odd = own % 2 == 1
    order_part = jnp.where(odd, half_turn(order_part), order_part)
    place_part = jnp.where(odd, place_part, half_turn(place_part))
    indices = jnp.where(upper, place_part, order_part)

    pitch = order_row(whole) + 1
    slots = out_ref.shape[0] // pitch
    for first in range(0, slots, ROWS):
        out_ref[pl.ds(pitch * first + far_row(whole), ROWS, stride=pitch), :] = far_col
        out_ref[pl.ds(pitch * first + order_row(whole), ROWS, stride=pitch), :] = indices
    copies[3].wait()
    parts = []
    for pair in range(variables // 2):
        fields = jnp.concatenate(
            [
                state_ref[:, pair].reshape(elements * nodes, levels),
                state_ref[:, variables // 2 + pair].reshape(elements * nodes, levels),
            ],
            axis=0,
        )
        parts.append(fields.T)
    scatter_levels(out_ref, pitch, whole, parts, with_wind=True)
    copies[4].wait()


def tendency_kernel(
    got_ref,
    weight_ref,
    settled_ref,
    out_ref,
    partial_ref,
    field,
    linear,
    tend,
    moved,
    whole,
    share,
):
    tiles = field.shape[0]
    row = row_ids()
    lower = lane_ids() < LANES // 2
    wind_row = jnp.where(row < 2 * whole, row | 1, 2 * whole)
    unpack_pairs(got_ref, field)
    step = min(tiles, 16)

    def multiply(chunk):
        fields = field[pl.ds(chunk * step, step)].reshape(step * 2 * ROWS, LANES)
        high, low = in_two(fields)
        coarse, fine = weight_ref[0], weight_ref[1]
        result = jnp.dot(
            jnp.concatenate([high, low], axis=1),
            jnp.concatenate([coarse, coarse], axis=0),
            preferred_element_type=jnp.float32,
        ) + jnp.dot(high, fine, preferred_element_type=jnp.float32)
        linear[pl.ds(chunk * step, step)] = result.reshape(step, 2, ROWS, 2 * LANES)

    each(tiles // step, multiply, 1)

    def advance(q):
        before = jnp.where(q == 0, tiles - 1, q - 1)
        after = jnp.where(q == tiles - 1, 0, q + 1)
        high = field[q, 1]
        wind = jnp.take_along_axis(high, wind_row, axis=0, mode="promise_in_bounds")
        sums = [0.0, 0.0]
        for side in range(2):
            far = row_of(field[q, side], far_row(whole)).astype(jnp.int32)
            spot = far & (LANES - 1)
            inside = lax.shift_right_arithmetic(far, 7) == q
            for part in range(2):
                beside = jnp.where(lower, field[after, part], field[before, part])
                value = jnp.where(inside, pick(field[q, part], spot), pick(beside, spot))
                sums[part] = sums[part] + jnp.where(far >= 0, value, 0.0)
        for part in range(2):
            own = field[q, part]
            result = (
                linear[q, part, :, :LANES]
                + wind * linear[q, part, :, LANES:]
                + PENALTY * sums[part]
            )
            tend[q, part] = result
            partial_ref[q, part] = jnp.where(
                row < far_row(whole), own + TIME_STEP * result, own
            )

    each(tiles, advance)
    swap_groups(tend, moved, share)

    def arrange(p):
        order = row_of(field[p, 0], order_row(whole)).astype(jnp.int32)
        pack_pair(out_ref, p, far_row(whole), *reorder(moved, p // 2 * 2, order))

    each(tiles, arrange)


def in_two(values):
    high = values.astype(jnp.bfloat16)
    low = (values - high.astype(jnp.float32)).astype(jnp.bfloat16)
    return high, low


def three_products(left, right, dims):
    left_high, left_low = in_two(left)
    right_high, right_low = in_two(right)
    return sum(
        lax.dot_general(a, b, (dims, ((), ())), preferred_element_type=jnp.float32)
        for a, b in ((left_high, right_high), (left_high, right_low), (left_low, right_high))
    )


def pool_weights(step):
    wide = WIDE * LANES
    lane = lax.broadcasted_iota(jnp.int32, (wide, LANES), 1) % (LANES // 2)
    owner = lax.broadcasted_iota(jnp.int32, (wide, LANES), 0) // CCOL
    mean = 1.0 / (CCOL * TIME_STEP)
    return jnp.where(lane == (wide // CCOL) * step + owner, mean, 0.0).astype(jnp.bfloat16)


def pooled_sum(tiles, weights):
    joined = jnp.concatenate([jnp.concatenate(tile, axis=0) for tile in tiles], axis=1)
    rows = joined.shape[0]
    both = jnp.concatenate(in_two(joined), axis=0)
    result = jnp.dot(both, weights, preferred_element_type=jnp.float32)
    return result[:rows] + result[rows:]


def settle_kernel(
    cloud_hbm,
    down_hbm,
    up_hbm,
    base_ref,
    mean_ref,
    pool_ref,
    spread_ref,
    down_ref,
    up_ref,
    cloud_ref,
    sums,
    sems,
):
    columns, variables, deep = base_ref.shape[:3]
    clev = cloud_hbm.shape[0]
    plane = (columns + 1) * variables
    steps = columns // WIDE
    small = [
        pltpu.make_async_copy(down_hbm, down_ref, sems.at[columns // PIECE]),
        pltpu.make_async_copy(up_hbm, up_ref, sems.at[columns // PIECE + 1]),
    ]

    def fetch(step):
        here = pl.ds(PIECE * step, PIECE)
        return pltpu.make_async_copy(
            cloud_hbm.at[:, here], cloud_ref.at[pl.ds(1, clev), here], sems.at[step]
        )

    pieces = columns // PIECE
    for step in range(pieces):
        fetch(step).start()
    for copy in small:
        copy.start()
    flat_ref = cloud_ref.reshape((deep + 2) * plane, LANES)
    rim = jnp.zeros((plane, LANES), jnp.float32)
    flat_ref[0:plane] = rim
    for level in range(clev, deep + 1):
        flat_ref[(level + 1) * plane : (level + 2) * plane] = rim
    sums[...] = jnp.zeros_like(sums)
    column = lax.broadcasted_iota(jnp.int32, spread_ref.shape, 0) % LANES
    place = lax.broadcasted_iota(jnp.int32, spread_ref.shape, 1)
    column_of = (LANES // 2) * (place // LANES) + place % LANES // CCOL
    spread_ref[...] = jnp.where(column == column_of, 1.0, 0.0).astype(jnp.bfloat16)
    lane = lane_ids()
    start = lane // CCOL * CCOL
    next_lane = start + (lane + 1) % CCOL
    last_lane = start + (lane + CCOL - 1) % CCOL

    def tile(t):
        def load(level, variable):
            begin = (level + 1) * plane + variables * t + variable
            return flat_ref[pl.ds(begin, ROWS, stride=plane), :]

        changes = []
        winds = [
            (-CLOUD_ADVECT * TIME_STEP) * load(level, 3) for level in range(0, deep, ROWS)
        ]
        for variable in range(variables):
            for level in range(0, deep, ROWS):
                now = load(level, variable)
                ahead = pick(now, next_lane)
                behind = pick(now, last_lane)
                around = load(level - 1, variable) + load(level + 1, variable)
                change = winds[level // ROWS] * (ahead - behind) + (
                    CLOUD_DIFFUSE * TIME_STEP
                ) * (around - 2.0 * now)
                base = now + change
                base_ref[t, variable, level : level + ROWS, :] = base
                changes.append(RETAIN * base - now if variable == 2 else change)
        return changes

    def advance(step, carry):
        weights = pool_weights(step)
        pool_ref[step] = weights
        results = []
        for n in range(WIDE):
            if n % PIECE == 0:
                fetch((WIDE // PIECE) * step + n // PIECE).wait()
            results.append(tile(WIDE * step + n))
        sums[...] += pooled_sum(results, weights)
        return carry

    lax.fori_loop(0, steps, advance, 0)
    lower = lane_ids(deep) < LANES // 2
    for pair in range(2):
        mean_ref[pair] = jnp.where(
            lower,
            sums[deep * pair : deep * (pair + 1)],
            sums[deep * (2 + pair) : deep * (3 + pair)],
        )
    for copy in small:
        copy.wait()


def cloud_kernel(
    got_ref,
    base_ref,
    mean_ref,
    pool_ref,
    spread_ref,
    down_ref,
    up_ref,
    next_hbm,
    out_ref,
    forced,
    sums,
    next_ref,
    sem,
    whole,
):
    columns, variables, deep = base_ref.shape[:3]
    clev, levels = down_ref.shape
    plane = (columns + 1) * variables
    flat_ref = next_ref.reshape(clev * plane, LANES)
    steps = columns // WIDE
    half = LANES // 2
    fields = jnp.concatenate(gather_levels(got_ref, whole, levels), axis=1)
    forcing = three_products(TIME_STEP * down_ref[...], fields, ((1,), (0,)))
    for pair in range(2):
        forced[pair, 0:clev] = forcing[:, LANES * pair : LANES * pair + LANES]
        forced[pair, clev:deep] = jnp.zeros((deep - clev, LANES), jnp.float32)
    sums[...] = jnp.zeros_like(sums)
    high, low = in_two(jnp.concatenate([forced[0], forced[1]], axis=0))

    def tile(t):
        shift = LANES - (LANES // CCOL) * t
        turned = [pltpu.roll(values, shift, 1) for values in (high, low)]
        push = jnp.dot(
            jnp.concatenate(turned, axis=1).astype(jnp.bfloat16),
            spread_ref[...],
            preferred_element_type=jnp.float32,
        )
        results = []
        for level in range(0, deep, ROWS):
            moved = []
            for variable in range(variables):
                begin = deep * (variable % 2) + level
                lanes = LANES * (variable // 2)
                moved.append(
                    base_ref[t, variable, level : level + ROWS, :]
                    + push[begin : begin + ROWS, lanes : lanes + LANES]
                )
            excess = moved[1] - SATURATION_BASE * jnp.exp2((SATURATION_SLOPE * LOG2_E) * moved[0])
            soft = jnp.maximum(excess, 0.0) + jnp.log(1.0 + jnp.exp2(-LOG2_E * jnp.abs(excess)))
            condensed = CONDENSE_RATE * soft
            updated = (
                moved[0] + condensed,
                moved[1] - condensed,
                RETAIN * moved[2] + condensed,
                moved[3],
            )
            count = min(ROWS, clev - level)
            for variable in range(variables):
                begin = level * plane + variables * t + variable
                flat_ref[pl.ds(begin, count, stride=plane), :] = updated[variable][:count]
            results.append(condensed)
        return results

    def store(begin, count):
        here = pl.ds(begin, count)
        return pltpu.make_async_copy(next_ref.at[:, here], next_hbm.at[:, here], sem)

    def advance(step, carry):
        results = []
        for n in range(WIDE):
            results.append(tile(WIDE * step + n))
            if (n + 1) % PIECE == 0:
                store(WIDE * step + n + 1 - PIECE, PIECE).start()
        sums[...] += pooled_sum(results, pool_ref[step])
        return carry

    lax.fori_loop(0, steps, advance, 0)
    lower = lane_ids(clev) < half
    extra = sums[0:clev]
    share = 1.0 / TIME_STEP
    first = mean_ref[0, 0:clev] + jnp.where(lower, share, share * RETAIN) * forced[0, 0:clev]
    first = first + extra
    second = mean_ref[1, 0:clev] + share * forced[1, 0:clev] - jnp.where(lower, extra, 0.0)
    feedback = three_products(
        up_ref[...], jnp.concatenate([first, second], axis=1), ((0,), (0,))
    )
    scatter_levels(
        out_ref,
        far_row(whole),
        whole,
        [feedback[:, LANES * pair : LANES * pair + LANES] for pair in range(2)],
    )
    store(0, columns).wait()


def update_kernel(got_ref, partial_ref, out_ref, field, sorted_ref, whole, share):
    tiles = field.shape[0]
    rows = got_ref.shape[0] // (2 * tiles)
    unpack_pairs(got_ref, field)

    def collect(p):
        place = row_of(partial_ref[p, 1], order_row(whole)).astype(jnp.int32)
        for part, values in enumerate(reorder(field, p // 2 * 2, place)):
            sorted_ref[p, part] = values

    each(tiles, collect)
    swap_groups(sorted_ref, field, share)

    def finish(q):
        pack_pair(
            out_ref,
            q,
            rows,
            partial_ref[q, 0] + TIME_STEP * field[q, 0],
            partial_ref[q, 1] + TIME_STEP * field[q, 1],
        )

    each(tiles, finish)


def unpack_kernel(got_ref, state_ref, whole):
    elements, variables, nodes, levels = state_ref.shape
    for pair, by_level in enumerate(gather_levels(got_ref, whole, levels)):
        fields = by_level.T.reshape(2, elements, nodes, levels)
        state_ref[:, pair] = fields[0]
        state_ref[:, variables // 2 + pair] = fields[1]


def kernel_call(body, name, results, scratch, *operands, hbm_in=(), hbm_out=(), cost=None):
    spec = {True: pl.BlockSpec(memory_space=pltpu.HBM), False: pl.BlockSpec(memory_space=pltpu.VMEM)}
    operands = [
        pltpu.with_memory_space_constraint(value, pltpu.HBM) if n in hbm_in else value
        for n, value in enumerate(operands)
    ]
    return pl.pallas_call(
        body,
        name=name,
        out_shape=results,
        in_specs=[spec[n in hbm_in] for n in range(len(operands))],
        out_specs=tuple(spec[n in hbm_out] for n in range(len(results))),
        scratch_shapes=scratch,
        cost_estimate=cost,
        compiler_params=pltpu.CompilerParams(vmem_limit_bytes=KERNEL_VMEM),
    )(*operands)


def exchange(values, devices):
    slots = values.reshape(devices, values.shape[0] // devices, 1, LANES)
    moved = lax.all_to_all(slots, AXES, split_axis=0, concat_axis=0, tiled=True)
    return moved.reshape(values.shape)


def shards(
    model_state,
    cloud_state,
    neighbor,
    facing_edge,
    column_order,
    model_to_cloud_levels,
    cloud_to_model_levels,
):
    elements, variables, nodes, levels = model_state.shape
    clev, width = cloud_state.shape[1:]
    devices = lax.axis_size(AXES)
    block = column_order.shape[1]
    share = block // lax.axis_size("cols")
    whole = levels // devices
    left = levels - whole * devices
    assert variables == 4 and nodes == NODES and 2 * elements * nodes == LANES
    assert variables * left <= devices and left % ROWS == 0 and devices % ROWS == 0
    assert order_row(whole) < ROWS and block == 2 * LANES
    tiles = devices // 2
    f32 = jnp.float32
    shape = jax.ShapeDtypeStruct
    flat = shape((devices * (order_row(whole) + 1), LANES), f32)
    rows = shape((devices * far_row(whole), LANES), f32)
    pairs = shape((tiles, 2, ROWS, LANES), f32)
    columns = width // LANES
    assert columns % WIDE == 0 and WIDE % PIECE == 0
    deep = -(-clev // ROWS) * ROWS
    dma = pltpu.SemaphoreType.DMA

    packed, weights = kernel_call(
        functools.partial(pack_kernel, whole=whole, block=block),
        "pack_state",
        (flat, shape((2, LANES, 2 * LANES), jnp.bfloat16)),
        [
            pltpu.SMEM(neighbor.shape, jnp.int32),
            pltpu.SMEM(facing_edge.shape, jnp.int32),
            pltpu.VMEM(column_order.shape, jnp.int32),
            pltpu.VMEM(model_state.shape, f32),
            pltpu.VMEM((2, ROWS, block), f32),
            dma((5,)),
        ],
        neighbor,
        facing_edge,
        column_order,
        model_state,
        node_weights(),
        hbm_in=range(5),
    )
    by_level = exchange(packed, devices)
    by_tile = cloud_state.reshape(variables, clev, columns, LANES).transpose(1, 2, 0, 3)
    base, mean, pool, spread, down, up = kernel_call(
        settle_kernel,
        "settle",
        (
            shape((columns, variables, deep, LANES), f32),
            shape((2, deep, LANES), f32),
            shape((columns // WIDE, WIDE * LANES, LANES), jnp.bfloat16),
            shape((2 * LANES, 2 * LANES), jnp.bfloat16),
            shape((clev, levels), f32),
            shape((clev, levels), f32),
        ),
        [
            pltpu.VMEM((deep + 2, columns + 1, variables, LANES), f32),
            pltpu.VMEM((variables * deep, LANES), f32),
            dma((columns // PIECE + 2,)),
        ],
        by_tile,
        model_to_cloud_levels,
        cloud_to_model_levels.T,
        hbm_in=range(3),
        cost=pl.CostEstimate(flops=10**8, bytes_accessed=4 * 10**6, transcendentals=0),
    )
    arranged, partial = kernel_call(
        functools.partial(tendency_kernel, whole=whole, share=share),
        "tendency",
        (rows, pairs),
        [
            pltpu.VMEM(pairs.shape, f32),
            pltpu.VMEM((tiles, 2, ROWS, 2 * LANES), f32),
            pltpu.VMEM(pairs.shape, f32),
            pltpu.VMEM(pairs.shape, f32),
        ],
        by_level,
        weights,
        down,
    )
    by_column = exchange(arranged, devices)
    cloud_next, fed = kernel_call(
        functools.partial(cloud_kernel, whole=whole),
        "cloud",
        (shape(by_tile.shape, f32), rows),
        [
            pltpu.VMEM((2, deep, LANES), f32),
            pltpu.VMEM((deep, LANES), f32),
            pltpu.VMEM((clev, columns + 1, variables, LANES), f32),
            dma,
        ],
        by_column,
        base,
        mean,
        pool,
        spread,
        down,
        up,
        hbm_out=(0,),
    )
    fed_level = exchange(fed, devices)
    (advanced,) = kernel_call(
        functools.partial(update_kernel, whole=whole, share=share),
        "update",
        (rows,),
        [pltpu.VMEM(pairs.shape, f32), pltpu.VMEM(pairs.shape, f32)],
        fed_level,
        partial,
    )
    home = exchange(advanced, devices)
    (model_next,) = kernel_call(
        functools.partial(unpack_kernel, whole=whole),
        "unpack_state",
        (shape(model_state.shape, f32),),
        [],
        home,
    )
    cloud_next = cloud_next.transpose(2, 0, 1, 3).reshape(cloud_state.shape)
    return (model_next, cloud_next)


def solution(mesh):
    placed = (
        P(AXES, None, None, None),
        P(None, None, AXES),
        P(AXES, None),
        P(AXES, None),
        P("cols", None),
        P(),
        P(),
    )
    return jax.shard_map(
        shards,
        mesh=mesh,
        in_specs=placed,
        out_specs=(P(AXES, None, None, None), P(None, None, AXES)),
        check_vma=False,
    )
```
